128 devices in a mesh: img: 16 (over z, x), pen: 8 (over y, core).
Axes of the slice: x: 4, y: 4, z: 4, core: 2. Of those that a mesh axis runs over, the one named last changes fastest.
Arguments:
- slice_tiles: bfloat16 [8192, 128, 256], P(('img', 'pen')), may hold values from -192 to 192
- ctf_tiles: bfloat16 [8192, 128, 128], P(('img', 'pen')), may hold values from 0.25 to 16
- entry_tile: int32 [16384], P(('img', 'pen')), may hold values from 0 to 63
- entry_brick: int32 [16384, 1], P(('img', 'pen')), may hold values from 0 to 127; in each aligned block of 128 rows (0 to 127, 128 to 255, ...) at most 2 rows name the same one
- entry_kernel: int32 [16384], P(('img', 'pen')), may hold values from 0 to 15
- ky_bank: bfloat16 [16, 48, 128], replicated, may hold values from 0 to 1
- kx_bank: bfloat16 [16, 128, 384], replicated, may hold values from 0 to 1
- z_bank: bfloat16 [16, 128], replicated, may hold values from 0.099609375 to 1
Outputs:
- volume: float32 [768, 768, 128], P('pen', 'img')
The draws below stay inside these ranges and needn't reach their ends.
Inputs may be any that keep to these rules, and one draw needn't show every extreme that they name: `entry_brick`: within the rows of one device no brick is named more than 2 times, a bound that some block reaches. `entry_tile`: an index among the 64 tiles of the entry's own device.
All inputs are finite; a program needn't handle non-finite values.
Results may differ from the reference program's by a relative error of at most 0.0041.
Values may be sent and summed in bfloat16 or wider, within the bound.
A program may use at most 192 MiB of HBM per device.

```python
import math
import jax
import jax.numpy as jnp
import numpy as np
from jax import lax

NBOX = 768
KXH = 384
PIX = 128
NK = 16
CAP = 2
KZD = 16
ZW = 128
KYB = 48
KZW = 128
ENTRIES_DEV = 128
TILES_DEV = 64
ENTRIES = 16384
TILES = 8192
N_IMG = 16
N_PEN = 8
DEVICES = 128


def draw_ctf_tiles(key, part):
    keys = jax.random.split(jax.random.fold_in(key, 11), 4)
    coord = (jnp.arange(PIX, dtype=jnp.float32) + 0.5) / PIX
    rows = coord[:, None]
    cols = coord[None, :]
    radius = jnp.sqrt(rows * rows + cols * cols)
    theta = jnp.arctan2(cols, rows)
    tilt = jax.random.uniform(keys[0], (), minval=0.0, maxval=math.pi)
    astig = 1.0 + 0.15 * jnp.cos(2.0 * (theta - tilt))
    defocus = 1.0 + 0.04 * jax.random.uniform(keys[1], (TILES, 1, 1), minval=-1.0, maxval=1.0)
    amplitude = jnp.exp(jax.random.uniform(keys[2], (TILES, 1, 1), minval=math.log(0.5), maxval=0.0))
    cycles = 3.0
    rough = jax.random.uniform(keys[3], (TILES, PIX, PIX), minval=0.5, maxval=1.0)
    wave = jnp.sin(math.pi * (cycles * radius * radius * astig * defocus + 0.1))
    envelope = jnp.exp(-1.2 * radius)
    return (0.25 + 15.75 * amplitude * envelope * (wave * wave) * rough).astype(jnp.bfloat16)


def banded(key, kernels, outer, inner, ratio, widen):
    keys = jax.random.split(key, 2)
    offset = jax.random.randint(keys[0], (kernels, 1, 1), -1, 2).astype(jnp.float32)
    half = 0.5 * ratio + widen
    center = (jnp.arange(outer, dtype=jnp.float32)[None, :, None] + 0.5) * ratio - 0.5 + offset
    center = jnp.clip(center, 0.0, inner - 1.0)
    distance = jnp.abs(jnp.arange(inner, dtype=jnp.float32)[None, None, :] - center)
    level = jnp.exp(jax.random.uniform(keys[1], (kernels, outer, inner), minval=math.log(0.5), maxval=math.log(2.0)))
    return jnp.where(distance <= half, level / (2.0 * half), 0.0)


def draw_ky_bank(key, part):
    return banded(jax.random.fold_in(key, 23), NK, KYB, PIX, PIX / KYB, 1.5).astype(jnp.bfloat16)


def draw_kx_bank(key, part):
    weights = banded(jax.random.fold_in(key, 37), NK, KXH, PIX, PIX / KXH, 1.0)
    return jnp.transpose(weights, (0, 2, 1)).astype(jnp.bfloat16)


def place_ends(result, key, least, largest):
    index_at = [jax.random.randint(jax.random.fold_in(key, axis), (), 0, length) for axis, length in enumerate(result.shape)]
    main_axis = result.shape.index(max(result.shape))
    neighbour = index_at[:main_axis] + [(index_at[main_axis] + 1) % result.shape[main_axis]] + index_at[main_axis + 1:]
    return result.at[tuple(index_at)].set(least).at[tuple(neighbour)].set(largest)


def shard_levels(key, extent, pieces, low, top_value):
    def one(position, shards_of):
        draws = jax.random.uniform(jax.random.fold_in(jax.random.fold_in(key, 6), position), (shards_of,), jnp.float32, low / len(pieces), top_value / len(pieces))
        return jnp.repeat(jnp.exp(draws), extent[position] // shards_of).reshape((-1,) + (1,) * (len(extent) - position - 1))

    loudness = one(*pieces[0])
    for cut in pieces[1:]:
        loudness = loudness * one(*cut)
    return loudness


def deal_out(own_key, own, number, rows, amount, top, most, slope):
    sequence = jax.random.permutation(own_key, amount)
    heavy_load, common = portions_of(amount, rows * top, most, slope, True), portions_of(amount, rows * top, most, slope, False)
    places = jnp.arange(amount)

    def named(lengths, rotation):
        used = int((lengths > 0).sum())
        fixed = max(1, used // 4)
        moved = fixed + (places - fixed + rotation * (used - fixed)) % max(1, amount - fixed)
        return jnp.zeros((amount,), jnp.int32).at[sequence[jnp.where(places < fixed, places, moved)]].set(jnp.asarray(lengths, jnp.int32))

    lengths = jnp.where(number % 4 == 0, named(heavy_load, number // 4), named(common, number - number // 4 - 1))
    mixed = jax.random.permutation(jax.random.fold_in(own, 3), amount)
    source_of, receiver = mixed[0:amount // 2 * 2:2], mixed[1:amount // 2 * 2:2]
    margin = jnp.minimum(lengths[source_of] - 1, most - lengths[receiver]) // 2
    margin = jnp.where((source_of == sequence[0]) | (receiver == sequence[0]) | (lengths[receiver] == 0), 0, jnp.maximum(margin, 0))
    moved = jax.random.randint(jax.random.fold_in(own, 4), (amount // 2,), 0, 1 << 20) % (margin + 1)
    lengths = lengths.at[source_of].add(-moved).at[receiver].add(moved)
    items = jnp.searchsorted(jnp.cumsum(lengths), jnp.arange(rows * top), side="right").astype(jnp.int32)
    listing = items.reshape(top, rows).T
    listing = listing[jax.random.permutation(jax.random.fold_in(own, 1), rows)]
    rotation = jax.random.randint(jax.random.fold_in(own, 2), (rows, 1), 0, top)
    return jnp.take_along_axis(listing, (jnp.arange(top)[None, :] + rotation) % top, axis=1)


def portions_of(amount, total, most, slope, full):
    loads = [(1 << 20) // math.isqrt(rank ** slope) + 1 for rank in range(1, amount + 1)]
    largest = most if full else min(most, max(-(-total // amount), total * loads[0] // sum(loads)))
    least = 1 if total - largest >= amount - 1 else 0
    counts, surplus = [largest] + [least] * (amount - 1), total - largest - least * (amount - 1)
    while surplus > 0:
        candidates = [i for i in range(1, amount) if counts[i] < largest] or [i for i in range(1, amount) if counts[i] < most]
        whole, left = sum([loads[i] for i in candidates]), surplus
        for i in candidates:
            addition = min(most - counts[i], max(1, left * loads[i] // whole), surplus)
            counts[i] = counts[i] + addition
            surplus = surplus - addition
    return np.array(counts)


def bell_draw(stream_key, extent, spread, bound, shards=(), held_as=jnp.bfloat16):
    result = spread * jax.random.normal(stream_key, extent, jnp.float32)
    if shards:
        result = result * shard_levels(stream_key, extent, shards, -0.22, 0.18)
    return jnp.clip(result, -bound, bound).astype(held_as)


def setup_inputs(seed: int = 0) -> dict:
    streams_of = jax.random.split(jax.random.key(seed), 9)
    slice_tiles = bell_draw(streams_of[0], (TILES, PIX, 2 * PIX), 32.0, 192.0, ((0, 128),))
    ctf_tiles = draw_ctf_tiles(jax.random.fold_in(streams_of[8], 71), 0)
    entry_tile = place_ends(jax.random.randint(streams_of[2], (ENTRIES,), 0, TILES_DEV), jax.random.fold_in(streams_of[2], 1), 0, TILES_DEV - 1).astype(jnp.int32)
    entry_brick_keys = jax.random.split(jax.random.fold_in(streams_of[3], 1), ENTRIES // ENTRIES_DEV)
    entry_brick_turns = jax.random.permutation(jax.random.fold_in(streams_of[3], 3), ENTRIES // ENTRIES_DEV)
    entry_brick = jax.vmap(lambda own, number: deal_out(jax.random.fold_in(streams_of[3], 2), own, number, ENTRIES_DEV, DEVICES, 1, CAP, 2))(entry_brick_keys, entry_brick_turns).reshape((ENTRIES, 1))
    entry_kernel = place_ends(jax.random.randint(streams_of[4], (ENTRIES,), 0, NK), jax.random.fold_in(streams_of[4], 1), 0, NK - 1).astype(jnp.int32)
    ky_bank = draw_ky_bank(jax.random.fold_in(streams_of[8], 71), 0)
    kx_bank = draw_kx_bank(jax.random.fold_in(streams_of[8], 71), 0)
    z_bank = jnp.clip(jnp.exp(jax.random.uniform(streams_of[7], (NK, KZW), jnp.float32, math.log(0.099609375), math.log(1.0))), 0.099609375, 1.0).astype(jnp.bfloat16)
    return {"slice_tiles": slice_tiles, "ctf_tiles": ctf_tiles, "entry_tile": entry_tile, "entry_brick": entry_brick, "entry_kernel": entry_kernel, "ky_bank": ky_bank, "kx_bank": kx_bank, "z_bank": z_bank}


def angle_table(left_idx, right_idx):
    product = left_idx[:, None] * right_idx[None, :] % NBOX
    return 2.0 * math.pi / NBOX * product.astype(jnp.float32)

def reference(slice_tiles, ctf_tiles, entry_tile, entry_brick, entry_kernel, ky_bank, kx_bank, z_bank):
    dev_count = N_IMG * N_PEN
    dest_brick = entry_brick[:, 0].reshape(dev_count, ENTRIES_DEV)
    tile_local = entry_tile.reshape(dev_count, ENTRIES_DEV)
    kernel_of = entry_kernel.reshape(dev_count, ENTRIES_DEV)
    positions = jnp.arange(ENTRIES_DEV, dtype=jnp.int32)
    same_brick = dest_brick[:, :, None] == dest_brick[:, None, :]
    before = positions[None, :] < positions[:, None]
    slot_rank = lax.optimization_barrier(jnp.sum((same_brick & before[None]).astype(jnp.int32), axis=2))
    tile_glob = tile_local + (jnp.arange(dev_count, dtype=jnp.int32) * TILES_DEV)[:, None]
    images = jnp.concatenate([slice_tiles, ctf_tiles], axis=2)
    slots = dev_count * CAP

    def owner_grid(brick):
        routed = dest_brick == brick
        hits = routed[:, :, None] & (slot_rank[:, :, None] == jnp.arange(CAP, dtype=jnp.int32)[None, None, :])
        entry_pos = lax.optimization_barrier(jnp.sum(jnp.where(hits, positions[None, :, None], 0), axis=1)).astype(jnp.int32)
        filled = jnp.any(hits, axis=1).reshape(-1)
        flat_pos = (jnp.arange(dev_count, dtype=jnp.int32)[:, None] * ENTRIES_DEV + entry_pos).reshape(-1)
        tiles_at = tile_glob.reshape(-1)[flat_pos]
        kernels_at = kernel_of.reshape(-1)[flat_pos]
        pixels = images[tiles_at].astype(jnp.float32)
        half_tile = jnp.einsum('syp,spc->syc', ky_bank[kernels_at].astype(jnp.float32), pixels, precision=lax.Precision.HIGHEST).astype(jnp.bfloat16)
        half_split = half_tile.astype(jnp.float32).reshape(slots, KYB, 3, PIX)
        full_tile = jnp.einsum('sycp,spq->sycq', half_split, kx_bank[kernels_at].astype(jnp.float32), precision=lax.Precision.HIGHEST).astype(jnp.bfloat16)
        full_tile = jnp.where(filled[:, None], full_tile.reshape(slots, -1), jnp.zeros((), jnp.bfloat16))
        z_columns = lax.dynamic_slice_in_dim(z_bank, (brick % N_PEN * KZD).astype(jnp.int32), KZD, 1)
        weights_z = z_columns[kernels_at]
        brick_sums = jnp.dot(weights_z.T, full_tile, preferred_element_type=jnp.float32).reshape(KZD, KYB, 3, KXH)
        denominator = brick_sums[:, :, 2] + 1.0
        return jnp.stack([brick_sums[:, :, 0] / denominator, brick_sums[:, :, 1] / denominator])
    owners = lax.map(owner_grid, jnp.arange(dev_count, dtype=jnp.int32))
    owners = owners.reshape(N_IMG, N_PEN, 2, KZD, KYB, KXH).transpose(2, 1, 3, 0, 4, 5).reshape(2, KZW, NBOX, KXH)
    grid_real, grid_imag = (owners[0], owners[1])
    angles = angle_table(jnp.arange(KZW, dtype=jnp.int32), jnp.arange(ZW, dtype=jnp.int32))
    cos_z, sin_z = (jnp.cos(angles), jnp.sin(angles))
    z_real = jnp.einsum('kyx,kz->zyx', grid_real, cos_z, precision=lax.Precision.HIGHEST) - jnp.einsum('kyx,kz->zyx', grid_imag, sin_z, precision=lax.Precision.HIGHEST)
    z_imag = jnp.einsum('kyx,kz->zyx', grid_real, sin_z, precision=lax.Precision.HIGHEST) + jnp.einsum('kyx,kz->zyx', grid_imag, cos_z, precision=lax.Precision.HIGHEST)
    spectrum = z_real + 1j * z_imag
    spectrum = jnp.fft.ifft(spectrum, axis=1) * NBOX
    spectrum = jnp.pad(spectrum, ((0, 0), (0, 0), (0, 1)))
    real_slab = jnp.fft.irfft(spectrum, n=NBOX, axis=2) * NBOX
    norm_scale = 1.0 / math.sqrt(KZW * NBOX * KXH)
    return (jnp.transpose(real_slab, (1, 2, 0)) * norm_scale).astype(jnp.float32)
```

```python
import math

import jax
import jax.numpy as jnp
from jax import lax
from jax.sharding import PartitionSpec as P

NBOX = 768
KXH = 384
PIX = 128
NK = 16
CAP = 2
ZW = 128


def angle_table(left_idx, right_idx):
    product = left_idx[:, None] * right_idx[None, :] % NBOX
    return 2.0 * math.pi / NBOX * product.astype(jnp.float32)


def local(slice_tiles, ctf_tiles, entry_tile, entry_brick, entry_kernel, ky_bank, kx_bank, z_bank):
    img_count = lax.axis_size("img")
    pen_count = lax.axis_size("pen")
    bricks = img_count * pen_count
    entry_count = entry_tile.shape[0]
    rows_brick = ky_bank.shape[1]
    window = z_bank.shape[1]
    planes = window // pen_count
    slot_total = bricks * CAP
    target = entry_brick[:, 0]
    positions = jnp.arange(entry_count, dtype=jnp.int32)
    earlier = (target[None, :] == target[:, None]) & (positions[None, :] < positions[:, None])
    slot_rank = jnp.sum(earlier.astype(jnp.int32), axis=1)
    slot_index = target * CAP + slot_rank
    owner = jnp.full((slot_total,), entry_count, jnp.int32).at[slot_index].set(positions)
    filled = owner < entry_count
    source = jnp.minimum(owner, entry_count - 1)
    tile_of = entry_tile[source]
    kernel_of = jnp.where(filled, entry_kernel[source], 0)
    rows_ky = ky_bank[kernel_of] * filled[:, None, None].astype(ky_bank.dtype)
    half_slice = jnp.einsum(
        "syp,spc->syc", rows_ky, slice_tiles[tile_of], preferred_element_type=jnp.float32
    ).astype(jnp.bfloat16)
    half_ctf = jnp.einsum(
        "syp,spc->syc", rows_ky, ctf_tiles[tile_of], preferred_element_type=jnp.float32
    ).astype(jnp.bfloat16)
    outgoing = jnp.concatenate([half_slice, half_ctf], axis=2)
    incoming, kind_ids = (
        lax.all_to_all(outgoing, ("img", "pen"), split_axis=0, concat_axis=0, tiled=True),
        lax.all_to_all(kernel_of, ("img", "pen"), split_axis=0, concat_axis=0, tiled=True),
    )
    shaped = incoming.reshape(slot_total, rows_brick, 3, PIX)
    gridded = jnp.einsum(
        "sycp,spq->sycq", shaped, kx_bank[kind_ids], preferred_element_type=jnp.float32
    ).astype(jnp.bfloat16)
    plane_start = lax.axis_index("pen") * planes
    z_columns = lax.dynamic_slice_in_dim(z_bank, plane_start, planes, 1)
    onehot = (kind_ids[:, None] == jnp.arange(NK, dtype=jnp.int32)[None, :]).astype(jnp.bfloat16)
    weights_z = jnp.dot(onehot, z_columns, preferred_element_type=jnp.float32).astype(jnp.bfloat16)
    brick_sums = jnp.dot(
        weights_z.T, gridded.reshape(slot_total, -1), preferred_element_type=jnp.float32
    ).reshape(planes, rows_brick, 3, KXH)
    denominator = brick_sums[:, :, 2] + 1.0
    grid_real = brick_sums[:, :, 0] / denominator
    grid_imag = brick_sums[:, :, 1] / denominator
    kx_idx = jnp.arange(KXH, dtype=jnp.int32)
    box_idx = jnp.arange(NBOX, dtype=jnp.int32)
    angles_x = angle_table(kx_idx, box_idx)
    weight_x = jnp.where(kx_idx == 0, 1.0, 2.0).astype(jnp.float32)[:, None]
    cos_x = weight_x * jnp.cos(angles_x)
    sin_x = weight_x * jnp.sin(angles_x)
    table_x = jnp.concatenate(
        [jnp.stack([cos_x, sin_x], -1), jnp.stack([-sin_x, cos_x], -1)], 0
    ).reshape(2 * KXH, 2 * NBOX)
    angles_y = angle_table(box_idx, box_idx)
    cos_y = jnp.cos(angles_y)
    sin_y = jnp.sin(angles_y)
    table_y = jnp.stack([jnp.stack([cos_y, sin_y], -1), jnp.stack([-sin_y, cos_y], -1)], 1)
    angles_z = angle_table(jnp.arange(window, dtype=jnp.int32), jnp.arange(ZW, dtype=jnp.int32))
    table_z = jnp.stack([jnp.cos(angles_z), -jnp.sin(angles_z)], 1)
    norm_scale = 1.0 / math.sqrt(window * NBOX * KXH)
    stacked = jnp.concatenate([grid_real, grid_imag], axis=2).reshape(planes * rows_brick, 2 * KXH)
    after_x = jnp.dot(stacked, table_x, precision=lax.Precision.HIGHEST).reshape(
        planes, rows_brick, 2 * NBOX
    )
    block_in = lax.all_to_all(after_x, "img", split_axis=2, concat_axis=1, tiled=True)
    items = block_in.shape[0]
    shaped = block_in.reshape(items, NBOX, -1, 2)
    result = jnp.einsum("nkxc,kcyd->nyxd", shaped, table_y, precision=lax.Precision.HIGHEST)
    after_y = result.reshape(items, NBOX, -1)
    return (
        jnp.einsum(
            "kyxc,kcz->yxz",
            lax.all_to_all(
                after_y.reshape(planes, NBOX, -1, 2), "pen", split_axis=1, concat_axis=0, tiled=True
            ),
            table_z,
            precision=lax.Precision.HIGHEST,
        )
        * norm_scale
    )


def solution(mesh):
    return jax.shard_map(
        local,
        mesh=mesh,
        in_specs=(
            P(("img", "pen"), None, None),
            P(("img", "pen"), None, None),
            P(("img", "pen")),
            P(("img", "pen"), None),
            P(("img", "pen")),
            P(),
            P(),
            P(),
        ),
        out_specs=P("pen", "img", None),
        check_vma=False,
    )
```

```python
import math

import jax
import jax.numpy as jnp
from jax import lax
from jax.experimental import pallas as pl
from jax.sharding import PartitionSpec as P

NBOX = 768
KXH = 384
PIX = 128
NK = 16
CAP = 2
ZW = 128


def angle_table(left_idx, right_idx):
    product = left_idx[:, None] * right_idx[None, :] % NBOX
    return 2.0 * math.pi / NBOX * product.astype(jnp.float32)


def kx_kernel(h_ref, w_ref, o_ref):
    @pl.when(pl.program_id(0) == 0)
    def _():
        o_ref[...] = jnp.zeros(o_ref.shape, o_ref.dtype)

    h = h_ref[0]
    hi = h.astype(jnp.bfloat16)
    lo = (h - hi.astype(jnp.float32)).astype(jnp.bfloat16)
    w = w_ref[0]
    o_ref[...] += jnp.dot(hi, w, preferred_element_type=jnp.float32) + jnp.dot(
        lo, w, preferred_element_type=jnp.float32
    )


def apply_kx(per_kernel, kx_bank):
    kernels, rows, pix = per_kernel.shape
    cols = kx_bank.shape[2]
    return pl.pallas_call(
        kx_kernel,
        grid=(kernels,),
        in_specs=[
            pl.BlockSpec((1, rows, pix), lambda k: (k, 0, 0)),
            pl.BlockSpec((1, pix, cols), lambda k: (k, 0, 0)),
        ],
        out_specs=pl.BlockSpec((rows, cols), lambda k: (0, 0)),
        out_shape=jax.ShapeDtypeStruct((rows, cols), jnp.float32),
    )(per_kernel, kx_bank)


def local(slice_tiles, ctf_tiles, entry_tile, entry_brick, entry_kernel, ky_bank, kx_bank, z_bank):
    img_count = lax.axis_size("img")
    pen_count = lax.axis_size("pen")
    bricks = img_count * pen_count
    entry_count = entry_tile.shape[0]
    rows_brick = ky_bank.shape[1]
    window = z_bank.shape[1]
    planes = window // pen_count
    slot_total = bricks * CAP
    target = entry_brick[:, 0]
    positions = jnp.arange(entry_count, dtype=jnp.int32)
    earlier = (target[None, :] == target[:, None]) & (positions[None, :] < positions[:, None])
    slot_rank = jnp.sum(earlier.astype(jnp.int32), axis=1)
    slot_index = target * CAP + slot_rank
    owner = jnp.full((slot_total,), entry_count, jnp.int32).at[slot_index].set(positions)
    filled = owner < entry_count
    source = jnp.minimum(owner, entry_count - 1)
    tile_of = entry_tile[source]
    kernel_of = jnp.where(filled, entry_kernel[source], 0)
    rows_ky = ky_bank[kernel_of] * filled[:, None, None].astype(ky_bank.dtype)
    half_slice = jnp.einsum(
        "syp,spc->syc", rows_ky, slice_tiles[tile_of], preferred_element_type=jnp.float32
    ).astype(jnp.bfloat16)
    half_ctf = jnp.einsum(
        "syp,spc->syc", rows_ky, ctf_tiles[tile_of], preferred_element_type=jnp.float32
    ).astype(jnp.bfloat16)
    outgoing = jnp.concatenate([half_slice, half_ctf], axis=2)
    incoming, kind_ids = (
        lax.all_to_all(outgoing, ("img", "pen"), split_axis=0, concat_axis=0, tiled=True),
        lax.all_to_all(kernel_of, ("img", "pen"), split_axis=0, concat_axis=0, tiled=True),
    )
    plane_start = lax.axis_index("pen") * planes
    z_columns = lax.dynamic_slice_in_dim(z_bank, plane_start, planes, 1)
    onehot = (kind_ids[:, None] == jnp.arange(NK, dtype=jnp.int32)[None, :]).astype(jnp.bfloat16)
    mixing = (onehot[:, :, None] * z_columns[None, :, :]).reshape(slot_total, NK * planes)
    per_kernel = jnp.dot(
        mixing.T, incoming.reshape(slot_total, -1), preferred_element_type=jnp.float32
    ).reshape(NK, planes * rows_brick * 3, PIX)
    brick_sums = apply_kx(per_kernel, kx_bank).reshape(planes, rows_brick, 3, KXH)
    denominator = brick_sums[:, :, 2] + 1.0
    grid_real = brick_sums[:, :, 0] / denominator
    grid_imag = brick_sums[:, :, 1] / denominator
    kx_idx = jnp.arange(KXH, dtype=jnp.int32)
    box_idx = jnp.arange(NBOX, dtype=jnp.int32)
    angles_x = angle_table(kx_idx, box_idx)
    weight_x = jnp.where(kx_idx == 0, 1.0, 2.0).astype(jnp.float32)[:, None]
    cos_x = weight_x * jnp.cos(angles_x)
    sin_x = weight_x * jnp.sin(angles_x)
    table_x = jnp.concatenate(
        [jnp.stack([cos_x, sin_x], -1), jnp.stack([-sin_x, cos_x], -1)], 0
    ).reshape(2 * KXH, 2 * NBOX)
    angles_y = angle_table(box_idx, box_idx)
    cos_y = jnp.cos(angles_y)
    sin_y = jnp.sin(angles_y)
    table_y = jnp.stack([jnp.stack([cos_y, sin_y], -1), jnp.stack([-sin_y, cos_y], -1)], 1)
    angles_z = angle_table(jnp.arange(window, dtype=jnp.int32), jnp.arange(ZW, dtype=jnp.int32))
    table_z = jnp.stack([jnp.cos(angles_z), -jnp.sin(angles_z)], 1)
    norm_scale = 1.0 / math.sqrt(window * NBOX * KXH)
    stacked = jnp.concatenate([grid_real, grid_imag], axis=2).reshape(planes * rows_brick, 2 * KXH)
    after_x = jnp.dot(stacked, table_x, precision=lax.Precision.HIGH).reshape(
        planes, rows_brick, 2 * NBOX
    )
    block_in = lax.all_to_all(after_x, "img", split_axis=2, concat_axis=1, tiled=True)
    items = block_in.shape[0]
    shaped = block_in.reshape(items, NBOX, -1, 2)
    result = jnp.einsum("nkxc,kcyd->nyxd", shaped, table_y, precision=lax.Precision.HIGH)
    after_y = result.reshape(items, NBOX, -1)
    return (
        jnp.einsum(
            "kyxc,kcz->yxz",
            lax.all_to_all(
                after_y.reshape(planes, NBOX, -1, 2), "pen", split_axis=1, concat_axis=0, tiled=True
            ),
            table_z,
            precision=lax.Precision.HIGH,
        )
        * norm_scale
    )


def solution(mesh):
    return jax.shard_map(
        local,
        mesh=mesh,
        in_specs=(
            P(("img", "pen"), None, None),
            P(("img", "pen"), None, None),
            P(("img", "pen")),
            P(("img", "pen"), None),
            P(("img", "pen")),
            P(),
            P(),
            P(),
        ),
        out_specs=P("pen", "img", None),
        check_vma=False,
    )
```

```python
import math

import jax
import jax.numpy as jnp
from jax import lax
from jax.experimental import pallas as pl
from jax.sharding import PartitionSpec as P

NBOX = 768
KXH = 384
PIX = 128
NK = 16
CAP = 2
ZW = 128


def angle_table(left_idx, right_idx):
    product = left_idx[:, None] * right_idx[None, :] % NBOX
    return 2.0 * math.pi / NBOX * product.astype(jnp.float32)


def kx_kernel(h_ref, w_ref, o_ref):
    @pl.when(pl.program_id(0) == 0)
    def _():
        o_ref[...] = jnp.zeros(o_ref.shape, o_ref.dtype)

    h = h_ref[0]
    hi = h.astype(jnp.bfloat16)
    lo = (h - hi.astype(jnp.float32)).astype(jnp.bfloat16)
    w = w_ref[0]
    o_ref[...] += jnp.dot(hi, w, preferred_element_type=jnp.float32) + jnp.dot(
        lo, w, preferred_element_type=jnp.float32
    )


def apply_kx(per_kernel, kx_bank):
    kernels, rows, pix = per_kernel.shape
    cols = kx_bank.shape[2]
    return pl.pallas_call(
        kx_kernel,
        grid=(kernels,),
        in_specs=[
            pl.BlockSpec((1, rows, pix), lambda k: (k, 0, 0)),
            pl.BlockSpec((1, pix, cols), lambda k: (k, 0, 0)),
        ],
        out_specs=pl.BlockSpec((rows, cols), lambda k: (0, 0)),
        out_shape=jax.ShapeDtypeStruct((rows, cols), jnp.float32),
    )(per_kernel, kx_bank)


def local(slice_tiles, ctf_tiles, entry_tile, entry_brick, entry_kernel, ky_bank, kx_bank, z_bank):
    img_count = lax.axis_size("img")
    pen_count = lax.axis_size("pen")
    bricks = img_count * pen_count
    entry_count = entry_tile.shape[0]
    rows_brick = ky_bank.shape[1]
    window = z_bank.shape[1]
    planes = window // pen_count
    slot_total = bricks * CAP
    target = entry_brick[:, 0]
    positions = jnp.arange(entry_count, dtype=jnp.int32)
    earlier = (target[None, :] == target[:, None]) & (positions[None, :] < positions[:, None])
    slot_rank = jnp.sum(earlier.astype(jnp.int32), axis=1)
    slot_index = target * CAP + slot_rank
    owner = jnp.full((slot_total,), entry_count, jnp.int32).at[slot_index].set(positions)
    filled = owner < entry_count
    source = jnp.minimum(owner, entry_count - 1)
    tile_of = entry_tile[source]
    kernel_of = jnp.where(filled, entry_kernel[source], 0)
    rows_ky = ky_bank[kernel_of] * filled[:, None, None].astype(ky_bank.dtype)
    half_slice = jnp.einsum(
        "syp,spc->syc", rows_ky, slice_tiles[tile_of], preferred_element_type=jnp.float32
    ).astype(jnp.bfloat16)
    half_ctf = jnp.einsum(
        "syp,spc->syc", rows_ky, ctf_tiles[tile_of], preferred_element_type=jnp.float32
    ).astype(jnp.bfloat16)
    outgoing = jnp.concatenate([half_slice, half_ctf], axis=2)
    incoming, kind_ids = (
        lax.all_to_all(outgoing, ("img", "pen"), split_axis=0, concat_axis=0, tiled=True),
        lax.all_to_all(kernel_of, ("img", "pen"), split_axis=0, concat_axis=0, tiled=True),
    )
    plane_start = lax.axis_index("pen") * planes
    z_columns = lax.dynamic_slice_in_dim(z_bank, plane_start, planes, 1)
    onehot = (kind_ids[:, None] == jnp.arange(NK, dtype=jnp.int32)[None, :]).astype(jnp.bfloat16)
    mixing = (onehot[:, :, None] * z_columns[None, :, :]).reshape(slot_total, NK * planes)
    per_kernel = jnp.dot(
        mixing.T, incoming.reshape(slot_total, -1), preferred_element_type=jnp.float32
    ).reshape(NK, planes * rows_brick * 3, PIX)
    brick_sums = apply_kx(per_kernel, kx_bank).reshape(planes, rows_brick, 3, KXH)
    denominator = brick_sums[:, :, 2] + 1.0
    grid_real = brick_sums[:, :, 0] / denominator
    grid_imag = brick_sums[:, :, 1] / denominator
    quarter = NBOX // 4
    row_x = lax.broadcasted_iota(jnp.int32, (2 * NBOX, 2 * KXH), 0)
    col_x = lax.broadcasted_iota(jnp.int32, (2 * NBOX, 2 * KXH), 1)
    kx_of = col_x % KXH
    phase_x = (row_x // 2) * kx_of + quarter * (col_x // KXH - row_x % 2)
    table_x = jnp.where(kx_of == 0, 1.0, 2.0) * jnp.cos(
        2.0 * math.pi / NBOX * (phase_x % NBOX).astype(jnp.float32)
    )
    row_y = lax.broadcasted_iota(jnp.int32, (2 * NBOX, 2 * NBOX), 0)
    col_y = lax.broadcasted_iota(jnp.int32, (2 * NBOX, 2 * NBOX), 1)
    phase_y = (row_y // 2) * (col_y // 2) + quarter * (col_y % 2 - row_y % 2)
    table_y = jnp.cos(2.0 * math.pi / NBOX * (phase_y % NBOX).astype(jnp.float32))
    norm_scale = 1.0 / math.sqrt(window * NBOX * KXH)
    row_z = lax.broadcasted_iota(jnp.int32, (2 * window, ZW), 0)
    col_z = lax.broadcasted_iota(jnp.int32, (2 * window, ZW), 1)
    phase_z = (row_z // 2) * col_z + quarter * (row_z % 2)
    table_z = norm_scale * jnp.cos(2.0 * math.pi / NBOX * (phase_z % NBOX).astype(jnp.float32))
    contract_minor = (((1,), (1,)), ((), ()))
    stacked = jnp.concatenate([grid_real, grid_imag], axis=2).reshape(planes * rows_brick, 2 * KXH)
    after_x = lax.dot_general(
        table_x, stacked, contract_minor, precision=lax.Precision.HIGH
    ).reshape(img_count, -1, planes * rows_brick)
    block_in = lax.all_to_all(after_x, "img", split_axis=0, concat_axis=0, tiled=True)
    x_local = NBOX // img_count
    rows_y = (
        block_in.reshape(img_count, x_local, 2, planes, rows_brick)
        .transpose(3, 1, 0, 4, 2)
        .reshape(planes * x_local, 2 * NBOX)
    )
    after_y = lax.dot_general(
        table_y, rows_y, contract_minor, precision=lax.Precision.HIGH
    ).reshape(pen_count, -1, planes * x_local)
    block_z = lax.all_to_all(after_y, "pen", split_axis=0, concat_axis=0, tiled=True)
    y_local = NBOX // pen_count
    rows_z = (
        block_z.reshape(pen_count, y_local, 2, planes, x_local)
        .transpose(1, 4, 0, 3, 2)
        .reshape(y_local * x_local, 2 * window)
    )
    volume = jnp.dot(rows_z, table_z, precision=lax.Precision.HIGH)
    return volume.reshape(y_local, x_local, ZW)

def solution(mesh):
    return jax.shard_map(
        local,
        mesh=mesh,
        in_specs=(
            P(("img", "pen"), None, None),
            P(("img", "pen"), None, None),
            P(("img", "pen")),
            P(("img", "pen"), None),
            P(("img", "pen")),
            P(),
            P(),
            P(),
        ),
        out_specs=P("pen", "img", None),
        check_vma=False,
    )
```

```python
import math

import jax
import jax.numpy as jnp
from jax import lax
from jax.experimental import pallas as pl
from jax.sharding import PartitionSpec as P

NBOX = 768
KXH = 384
PIX = 128
NK = 16
CAP = 2
ZW = 128


def angle_table(left_idx, right_idx):
    product = left_idx[:, None] * right_idx[None, :] % NBOX
    return 2.0 * math.pi / NBOX * product.astype(jnp.float32)


def kx_kernel(h_ref, w_ref, o_ref):
    @pl.when(pl.program_id(0) == 0)
    def _():
        o_ref[...] = jnp.zeros(o_ref.shape, o_ref.dtype)

    h = h_ref[0]
    hi = h.astype(jnp.bfloat16)
    lo = (h - hi.astype(jnp.float32)).astype(jnp.bfloat16)
    w = w_ref[0]
    o_ref[...] += jnp.dot(hi, w, preferred_element_type=jnp.float32) + jnp.dot(
        lo, w, preferred_element_type=jnp.float32
    )


def apply_kx(per_kernel, kx_bank):
    kernels, rows, pix = per_kernel.shape
    cols = kx_bank.shape[2]
    return pl.pallas_call(
        kx_kernel,
        grid=(kernels,),
        in_specs=[
            pl.BlockSpec((1, rows, pix), lambda k: (k, 0, 0)),
            pl.BlockSpec((1, pix, cols), lambda k: (k, 0, 0)),
        ],
        out_specs=pl.BlockSpec((rows, cols), lambda k: (0, 0)),
        out_shape=jax.ShapeDtypeStruct((rows, cols), jnp.float32),
    )(per_kernel, kx_bank)


def local(slice_tiles, ctf_tiles, entry_tile, entry_brick, entry_kernel, ky_bank, kx_bank, z_bank):
    img_count = lax.axis_size("img")
    pen_count = lax.axis_size("pen")
    bricks = img_count * pen_count
    entry_count = entry_tile.shape[0]
    rows_brick = ky_bank.shape[1]
    window = z_bank.shape[1]
    planes = window // pen_count
    slot_total = bricks * CAP
    target = entry_brick[:, 0]
    positions = jnp.arange(entry_count, dtype=jnp.int32)
    earlier = (target[None, :] == target[:, None]) & (positions[None, :] < positions[:, None])
    slot_rank = jnp.sum(earlier.astype(jnp.int32), axis=1)
    slot_index = target * CAP + slot_rank
    owner = jnp.full((slot_total,), entry_count, jnp.int32).at[slot_index].set(positions)
    filled = owner < entry_count
    source = jnp.minimum(owner, entry_count - 1)
    tile_of = entry_tile[source]
    kernel_of = jnp.where(filled, entry_kernel[source], 0)
    rows_ky = ky_bank[kernel_of] * filled[:, None, None].astype(ky_bank.dtype)
    half_slice = jnp.einsum(
        "syp,spc->syc", rows_ky, slice_tiles[tile_of], preferred_element_type=jnp.float32
    ).astype(jnp.bfloat16)
    half_ctf = jnp.einsum(
        "syp,spc->syc", rows_ky, ctf_tiles[tile_of], preferred_element_type=jnp.float32
    ).astype(jnp.bfloat16)
    outgoing = jnp.concatenate([half_slice, half_ctf], axis=2)
    incoming, kind_ids = (
        lax.all_to_all(outgoing, ("img", "pen"), split_axis=0, concat_axis=0, tiled=True),
        lax.all_to_all(kernel_of, ("img", "pen"), split_axis=0, concat_axis=0, tiled=True),
    )
    plane_start = lax.axis_index("pen") * planes
    z_columns = lax.dynamic_slice_in_dim(z_bank, plane_start, planes, 1)
    onehot = (kind_ids[:, None] == jnp.arange(NK, dtype=jnp.int32)[None, :]).astype(jnp.bfloat16)
    mixing = (onehot[:, :, None] * z_columns[None, :, :]).reshape(slot_total, NK * planes)
    per_kernel = jnp.dot(
        mixing.T, incoming.reshape(slot_total, -1), preferred_element_type=jnp.float32
    ).reshape(NK, planes * rows_brick * 3, PIX)
    brick_sums = apply_kx(per_kernel, kx_bank).reshape(planes, rows_brick, 3, KXH)
    denominator = brick_sums[:, :, 2] + 1.0
    grid_real = brick_sums[:, :, 0] / denominator
    grid_imag = brick_sums[:, :, 1] / denominator
    quarter = NBOX // 4
    row_x = lax.broadcasted_iota(jnp.int32, (2 * NBOX, 2 * KXH), 0)
    col_x = lax.broadcasted_iota(jnp.int32, (2 * NBOX, 2 * KXH), 1)
    kx_of = col_x % KXH
    phase_x = (row_x // 2) * kx_of + quarter * (col_x // KXH - row_x % 2)
    table_x = jnp.where(kx_of == 0, 1.0, 2.0) * jnp.cos(
        2.0 * math.pi / NBOX * (phase_x % NBOX).astype(jnp.float32)
    )
    row_y = lax.broadcasted_iota(jnp.int32, (2 * NBOX, 2 * NBOX), 0)
    col_y = lax.broadcasted_iota(jnp.int32, (2 * NBOX, 2 * NBOX), 1)
    phase_y = (row_y // 2) * (col_y // 2) + quarter * (col_y % 2 - row_y % 2)
    table_y = jnp.cos(2.0 * math.pi / NBOX * (phase_y % NBOX).astype(jnp.float32))
    norm_scale = 1.0 / math.sqrt(window * NBOX * KXH)
    row_z = lax.broadcasted_iota(jnp.int32, (2 * window, ZW), 0)
    col_z = lax.broadcasted_iota(jnp.int32, (2 * window, ZW), 1)
    phase_z = (row_z // 2) * col_z + quarter * (row_z % 2)
    table_z = norm_scale * jnp.cos(2.0 * math.pi / NBOX * (phase_z % NBOX).astype(jnp.float32))
    table_x, table_y, table_z = lax.optimization_barrier((table_x, table_y, table_z))
    contract_minor = (((1,), (1,)), ((), ()))
    stacked = jnp.concatenate([grid_real, grid_imag], axis=2).reshape(planes * rows_brick, 2 * KXH)
    after_x = lax.dot_general(
        table_x, stacked, contract_minor, precision=lax.Precision.HIGH
    ).reshape(img_count, -1, planes * rows_brick)
    block_in = lax.all_to_all(after_x, "img", split_axis=0, concat_axis=0, tiled=True)
    x_local = NBOX // img_count
    rows_y = (
        block_in.reshape(img_count, x_local, 2, planes, rows_brick)
        .transpose(3, 1, 0, 4, 2)
        .reshape(planes * x_local, 2 * NBOX)
    )
    after_y = lax.dot_general(
        table_y, rows_y, contract_minor, precision=lax.Precision.HIGH
    ).reshape(pen_count, -1, planes * x_local)
    block_z = lax.all_to_all(after_y, "pen", split_axis=0, concat_axis=0, tiled=True)
    y_local = NBOX // pen_count
    rows_z = (
        block_z.reshape(pen_count, y_local, 2, planes, x_local)
        .transpose(1, 4, 0, 3, 2)
        .reshape(y_local * x_local, 2 * window)
    )
    volume = jnp.dot(rows_z, table_z, precision=lax.Precision.HIGH)
    return volume.reshape(y_local, x_local, ZW)

def solution(mesh):
    return jax.shard_map(
        local,
        mesh=mesh,
        in_specs=(
            P(("img", "pen"), None, None),
            P(("img", "pen"), None, None),
            P(("img", "pen")),
            P(("img", "pen"), None),
            P(("img", "pen")),
            P(),
            P(),
            P(),
        ),
        out_specs=P("pen", "img", None),
        check_vma=False,
    )
```

```python
import math

import jax
import jax.numpy as jnp
from jax import lax
from jax.experimental import pallas as pl
from jax.sharding import PartitionSpec as P

NBOX = 768
KXH = 384
PIX = 128
NK = 16
CAP = 2
ZW = 128


def angle_table(left_idx, right_idx):
    product = left_idx[:, None] * right_idx[None, :] % NBOX
    return 2.0 * math.pi / NBOX * product.astype(jnp.float32)


def kx_kernel(h_ref, w_ref, o_ref):
    @pl.when(pl.program_id(0) == 0)
    def _():
        o_ref[...] = jnp.zeros(o_ref.shape, o_ref.dtype)

    h = h_ref[0]
    hi = h.astype(jnp.bfloat16)
    lo = (h - hi.astype(jnp.float32)).astype(jnp.bfloat16)
    w = w_ref[0]
    o_ref[...] += jnp.dot(hi, w, preferred_element_type=jnp.float32) + jnp.dot(
        lo, w, preferred_element_type=jnp.float32
    )


def apply_kx(per_kernel, kx_bank):
    kernels, rows, pix = per_kernel.shape
    cols = kx_bank.shape[2]
    return pl.pallas_call(
        kx_kernel,
        grid=(kernels,),
        in_specs=[
            pl.BlockSpec((1, rows, pix), lambda k: (k, 0, 0)),
            pl.BlockSpec((1, pix, cols), lambda k: (k, 0, 0)),
        ],
        out_specs=pl.BlockSpec((rows, cols), lambda k: (0, 0)),
        out_shape=jax.ShapeDtypeStruct((rows, cols), jnp.float32),
    )(per_kernel, kx_bank)


def local(slice_tiles, ctf_tiles, entry_tile, entry_brick, entry_kernel, ky_bank, kx_bank, z_bank):
    img_count = lax.axis_size("img")
    pen_count = lax.axis_size("pen")
    bricks = img_count * pen_count
    entry_count = entry_tile.shape[0]
    rows_brick = ky_bank.shape[1]
    window = z_bank.shape[1]
    planes = window // pen_count
    slot_total = bricks * CAP
    target = entry_brick[:, 0]
    positions = jnp.arange(entry_count, dtype=jnp.int32)
    earlier = (target[None, :] == target[:, None]) & (positions[None, :] < positions[:, None])
    slot_rank = jnp.sum(earlier.astype(jnp.int32), axis=1)
    slot_index = target * CAP + slot_rank
    owner = jnp.full((slot_total,), entry_count, jnp.int32).at[slot_index].set(positions)
    owner = owner.reshape(bricks, CAP)
    plane_start = lax.axis_index("pen") * planes
    z_columns = lax.dynamic_slice_in_dim(z_bank, plane_start, planes, 1)
    per_kernel = None
    for rank in range(CAP):
        owned = owner[:, rank]
        filled = owned < entry_count
        source = jnp.minimum(owned, entry_count - 1)
        tile_of = entry_tile[source]
        kernel_of = jnp.where(filled, entry_kernel[source], 0)
        rows_ky = ky_bank[kernel_of] * filled[:, None, None].astype(ky_bank.dtype)
        half_slice = jnp.einsum(
            "syp,spc->syc", rows_ky, slice_tiles[tile_of], preferred_element_type=jnp.float32
        ).astype(jnp.bfloat16)
        half_ctf = jnp.einsum(
            "syp,spc->syc", rows_ky, ctf_tiles[tile_of], preferred_element_type=jnp.float32
        ).astype(jnp.bfloat16)
        outgoing = jnp.concatenate([half_slice, half_ctf], axis=2)
        incoming, kind_ids = (
            lax.all_to_all(outgoing, ("img", "pen"), split_axis=0, concat_axis=0, tiled=True),
            lax.all_to_all(kernel_of, ("img", "pen"), split_axis=0, concat_axis=0, tiled=True),
        )
        onehot = (kind_ids[:, None] == jnp.arange(NK, dtype=jnp.int32)[None, :]).astype(jnp.bfloat16)
        mixing = (onehot[:, :, None] * z_columns[None, :, :]).reshape(bricks, NK * planes)
        part = jnp.dot(mixing.T, incoming.reshape(bricks, -1), preferred_element_type=jnp.float32)
        per_kernel = part if per_kernel is None else per_kernel + part
    per_kernel = per_kernel.reshape(NK, planes * rows_brick * 3, PIX)
    brick_sums = apply_kx(per_kernel, kx_bank).reshape(planes, rows_brick, 3, KXH)
    denominator = brick_sums[:, :, 2] + 1.0
    grid_real = brick_sums[:, :, 0] / denominator
    grid_imag = brick_sums[:, :, 1] / denominator
    quarter = NBOX // 4
    row_x = lax.broadcasted_iota(jnp.int32, (2 * NBOX, 2 * KXH), 0)
    col_x = lax.broadcasted_iota(jnp.int32, (2 * NBOX, 2 * KXH), 1)
    kx_of = col_x % KXH
    phase_x = (row_x // 2) * kx_of + quarter * (col_x // KXH - row_x % 2)
    table_x = jnp.where(kx_of == 0, 1.0, 2.0) * jnp.cos(
        2.0 * math.pi / NBOX * (phase_x % NBOX).astype(jnp.float32)
    )
    row_y = lax.broadcasted_iota(jnp.int32, (2 * NBOX, 2 * NBOX), 0)
    col_y = lax.broadcasted_iota(jnp.int32, (2 * NBOX, 2 * NBOX), 1)
    phase_y = (row_y // 2) * (col_y // 2) + quarter * (col_y % 2 - row_y % 2)
    table_y = jnp.cos(2.0 * math.pi / NBOX * (phase_y % NBOX).astype(jnp.float32))
    norm_scale = 1.0 / math.sqrt(window * NBOX * KXH)
    row_z = lax.broadcasted_iota(jnp.int32, (2 * window, ZW), 0)
    col_z = lax.broadcasted_iota(jnp.int32, (2 * window, ZW), 1)
    phase_z = (row_z // 2) * col_z + quarter * (row_z % 2)
    table_z = norm_scale * jnp.cos(2.0 * math.pi / NBOX * (phase_z % NBOX).astype(jnp.float32))
    table_x, table_y, table_z = lax.optimization_barrier((table_x, table_y, table_z))
    contract_minor = (((1,), (1,)), ((), ()))
    stacked = jnp.concatenate([grid_real, grid_imag], axis=2).reshape(planes * rows_brick, 2 * KXH)
    after_x = lax.dot_general(
        table_x, stacked, contract_minor, precision=lax.Precision.HIGH
    ).reshape(img_count, -1, planes * rows_brick)
    block_in = lax.all_to_all(after_x, "img", split_axis=0, concat_axis=0, tiled=True)
    x_local = NBOX // img_count
    rows_y = (
        block_in.reshape(img_count, x_local, 2, planes, rows_brick)
        .transpose(3, 1, 0, 4, 2)
        .reshape(planes * x_local, 2 * NBOX)
    )
    after_y = lax.dot_general(
        table_y, rows_y, contract_minor, precision=lax.Precision.HIGH
    ).reshape(pen_count, -1, planes * x_local)
    block_z = lax.all_to_all(after_y, "pen", split_axis=0, concat_axis=0, tiled=True)
    y_local = NBOX // pen_count
    rows_z = (
        block_z.reshape(pen_count, y_local, 2, planes, x_local)
        .transpose(1, 4, 0, 3, 2)
        .reshape(y_local * x_local, 2 * window)
    )
    volume = jnp.dot(rows_z, table_z, precision=lax.Precision.HIGH)
    return volume.reshape(y_local, x_local, ZW)

def solution(mesh):
    return jax.shard_map(
        local,
        mesh=mesh,
        in_specs=(
            P(("img", "pen"), None, None),
            P(("img", "pen"), None, None),
            P(("img", "pen")),
            P(("img", "pen"), None),
            P(("img", "pen")),
            P(),
            P(),
            P(),
        ),
        out_specs=P("pen", "img", None),
        check_vma=False,
    )
```

```python
import math

import jax
import jax.numpy as jnp
from jax import lax
from jax.experimental import pallas as pl
from jax.sharding import PartitionSpec as P

NBOX = 768
KXH = 384
PIX = 128
NK = 16
CAP = 2
ZW = 128


def angle_table(left_idx, right_idx):
    product = left_idx[:, None] * right_idx[None, :] % NBOX
    return 2.0 * math.pi / NBOX * product.astype(jnp.float32)


def kx_kernel(h_ref, w_ref, o_ref):
    @pl.when(pl.program_id(0) == 0)
    def _():
        o_ref[...] = jnp.zeros(o_ref.shape, o_ref.dtype)

    pix = w_ref.shape[1]
    h = jnp.concatenate(
        [h_ref[:, m * pix:(m + 1) * pix] for m in range(h_ref.shape[1] // pix)], axis=0
    )
    hi = h.astype(jnp.bfloat16)
    lo = (h - hi.astype(jnp.float32)).astype(jnp.bfloat16)
    w = w_ref[0]
    o_ref[...] += jnp.dot(hi, w, preferred_element_type=jnp.float32) + jnp.dot(
        lo, w, preferred_element_type=jnp.float32
    )


def apply_kx(per_kernel, kx_bank):
    kernels, pix, cols = kx_bank.shape
    planes = per_kernel.shape[0] // kernels
    width = per_kernel.shape[1]
    rows = planes * width // pix
    return pl.pallas_call(
        kx_kernel,
        grid=(kernels,),
        in_specs=[
            pl.BlockSpec((planes, width), lambda k: (k, 0)),
            pl.BlockSpec((1, pix, cols), lambda k: (k, 0, 0)),
        ],
        out_specs=pl.BlockSpec((rows, cols), lambda k: (0, 0)),
        out_shape=jax.ShapeDtypeStruct((rows, cols), jnp.float32),
    )(per_kernel, kx_bank)

def local(slice_tiles, ctf_tiles, entry_tile, entry_brick, entry_kernel, ky_bank, kx_bank, z_bank):
    img_count = lax.axis_size("img")
    pen_count = lax.axis_size("pen")
    bricks = img_count * pen_count
    entry_count = entry_tile.shape[0]
    rows_brick = ky_bank.shape[1]
    window = z_bank.shape[1]
    planes = window // pen_count
    slot_total = bricks * CAP
    target = entry_brick[:, 0]
    positions = jnp.arange(entry_count, dtype=jnp.int32)
    earlier = (target[None, :] == target[:, None]) & (positions[None, :] < positions[:, None])
    slot_rank = jnp.sum(earlier.astype(jnp.int32), axis=1)
    slot_index = target * CAP + slot_rank
    owner = jnp.full((slot_total,), entry_count, jnp.int32).at[slot_index].set(positions)
    filled = owner < entry_count
    source = jnp.minimum(owner, entry_count - 1)
    tile_of = entry_tile[source]
    kernel_of = jnp.where(filled, entry_kernel[source], 0)
    rows_ky = ky_bank[kernel_of] * filled[:, None, None].astype(ky_bank.dtype)
    half_slice = jnp.einsum(
        "syp,spc->syc", rows_ky, slice_tiles[tile_of], preferred_element_type=jnp.float32
    ).astype(jnp.bfloat16)
    half_ctf = jnp.einsum(
        "syp,spc->syc", rows_ky, ctf_tiles[tile_of], preferred_element_type=jnp.float32
    ).astype(jnp.bfloat16)
    outgoing = jnp.concatenate([half_slice, half_ctf], axis=2)
    incoming, kind_ids = (
        lax.all_to_all(outgoing, ("img", "pen"), split_axis=0, concat_axis=0, tiled=True),
        lax.all_to_all(kernel_of, ("img", "pen"), split_axis=0, concat_axis=0, tiled=True),
    )
    plane_start = lax.axis_index("pen") * planes
    z_columns = lax.dynamic_slice_in_dim(z_bank, plane_start, planes, 1)
    onehot = (kind_ids[:, None] == jnp.arange(NK, dtype=jnp.int32)[None, :]).astype(jnp.bfloat16)
    mixing = (onehot[:, :, None] * z_columns[None, :, :]).reshape(slot_total, NK * planes)
    per_kernel = jnp.dot(
        mixing.T, incoming.reshape(slot_total, -1), preferred_element_type=jnp.float32
    )
    brick_sums = apply_kx(per_kernel, kx_bank).reshape(rows_brick, 3, planes, KXH)
    denominator = brick_sums[:, 2] + 1.0
    grid_real = brick_sums[:, 0] / denominator
    grid_imag = brick_sums[:, 1] / denominator
    quarter = NBOX // 4
    row_x = lax.broadcasted_iota(jnp.int32, (2 * NBOX, 2 * KXH), 0)
    col_x = lax.broadcasted_iota(jnp.int32, (2 * NBOX, 2 * KXH), 1)
    kx_of = col_x % KXH
    phase_x = (row_x // 2) * kx_of + quarter * (col_x // KXH - row_x % 2)
    table_x = jnp.where(kx_of == 0, 1.0, 2.0) * jnp.cos(
        2.0 * math.pi / NBOX * (phase_x % NBOX).astype(jnp.float32)
    )
    row_y = lax.broadcasted_iota(jnp.int32, (2 * NBOX, 2 * NBOX), 0)
    col_y = lax.broadcasted_iota(jnp.int32, (2 * NBOX, 2 * NBOX), 1)
    phase_y = (row_y // 2) * (col_y // 2) + quarter * (col_y % 2 - row_y % 2)
    table_y = jnp.cos(2.0 * math.pi / NBOX * (phase_y % NBOX).astype(jnp.float32))
    norm_scale = 1.0 / math.sqrt(window * NBOX * KXH)
    row_z = lax.broadcasted_iota(jnp.int32, (2 * window, ZW), 0)
    col_z = lax.broadcasted_iota(jnp.int32, (2 * window, ZW), 1)
    phase_z = (row_z // 2) * col_z + quarter * (row_z % 2)
    table_z = norm_scale * jnp.cos(2.0 * math.pi / NBOX * (phase_z % NBOX).astype(jnp.float32))
    table_x, table_y, table_z = lax.optimization_barrier((table_x, table_y, table_z))
    contract_minor = (((1,), (1,)), ((), ()))
    stacked = jnp.concatenate([grid_real, grid_imag], axis=2).reshape(planes * rows_brick, 2 * KXH)
    after_x = lax.dot_general(
        table_x, stacked, contract_minor, precision=lax.Precision.HIGH
    ).reshape(img_count, -1, planes * rows_brick)
    block_in = lax.all_to_all(after_x, "img", split_axis=0, concat_axis=0, tiled=True)
    x_local = NBOX // img_count
    rows_y = (
        block_in.reshape(img_count, x_local, 2, rows_brick, planes)
        .transpose(4, 1, 0, 3, 2)
        .reshape(planes * x_local, 2 * NBOX)
    )
    after_y = lax.dot_general(
        table_y, rows_y, contract_minor, precision=lax.Precision.HIGH
    ).reshape(pen_count, -1, planes * x_local)
    block_z = lax.all_to_all(after_y, "pen", split_axis=0, concat_axis=0, tiled=True)
    y_local = NBOX // pen_count
    rows_z = (
        block_z.reshape(pen_count, y_local, 2, planes, x_local)
        .transpose(1, 4, 0, 3, 2)
        .reshape(y_local * x_local, 2 * window)
    )
    volume = jnp.dot(rows_z, table_z, precision=lax.Precision.HIGH)
    return volume.reshape(y_local, x_local, ZW)

def solution(mesh):
    return jax.shard_map(
        local,
        mesh=mesh,
        in_specs=(
            P(("img", "pen"), None, None),
            P(("img", "pen"), None, None),
            P(("img", "pen")),
            P(("img", "pen"), None),
            P(("img", "pen")),
            P(),
            P(),
            P(),
        ),
        out_specs=P("pen", "img", None),
        check_vma=False,
    )
```

```python
import math

import jax
import jax.numpy as jnp
from jax import lax
from jax.experimental import pallas as pl
from jax.sharding import PartitionSpec as P

NBOX = 768
KXH = 384
PIX = 128
NK = 16
CAP = 2
ZW = 128


def angle_table(left_idx, right_idx):
    product = left_idx[:, None] * right_idx[None, :] % NBOX
    return 2.0 * math.pi / NBOX * product.astype(jnp.float32)


def kx_kernel(h_ref, w_ref, o_ref):
    @pl.when(pl.program_id(0) == 0)
    def _():
        o_ref[...] = jnp.zeros(o_ref.shape, o_ref.dtype)

    pix = w_ref.shape[1]
    h = jnp.concatenate(
        [h_ref[:, m * pix:(m + 1) * pix] for m in range(h_ref.shape[1] // pix)], axis=0
    )
    hi = h.astype(jnp.bfloat16)
    lo = (h - hi.astype(jnp.float32)).astype(jnp.bfloat16)
    w = w_ref[0]
    o_ref[...] += jnp.dot(hi, w, preferred_element_type=jnp.float32) + jnp.dot(
        lo, w, preferred_element_type=jnp.float32
    )


def apply_kx(per_kernel, kx_bank):
    kernels, pix, cols = kx_bank.shape
    planes = per_kernel.shape[0] // kernels
    width = per_kernel.shape[1]
    rows = planes * width // pix
    return pl.pallas_call(
        kx_kernel,
        grid=(kernels,),
        in_specs=[
            pl.BlockSpec((planes, width), lambda k: (k, 0)),
            pl.BlockSpec((1, pix, cols), lambda k: (k, 0, 0)),
        ],
        out_specs=pl.BlockSpec((rows, cols), lambda k: (0, 0)),
        out_shape=jax.ShapeDtypeStruct((rows, cols), jnp.float32),
    )(per_kernel, kx_bank)

def local(slice_tiles, ctf_tiles, entry_tile, entry_brick, entry_kernel, ky_bank, kx_bank, z_bank):
    img_count = lax.axis_size("img")
    pen_count = lax.axis_size("pen")
    bricks = img_count * pen_count
    entry_count = entry_tile.shape[0]
    rows_brick = ky_bank.shape[1]
    window = z_bank.shape[1]
    planes = window // pen_count
    slot_total = bricks * CAP
    target = entry_brick[:, 0]
    positions = jnp.arange(entry_count, dtype=jnp.int32)
    earlier = (target[None, :] == target[:, None]) & (positions[None, :] < positions[:, None])
    slot_rank = jnp.sum(earlier.astype(jnp.int32), axis=1)
    slot_index = target * CAP + slot_rank
    owner = jnp.full((slot_total,), entry_count, jnp.int32).at[slot_index].set(positions)
    filled = owner < entry_count
    source = jnp.minimum(owner, entry_count - 1)
    tile_of = entry_tile[source]
    kernel_of = jnp.where(filled, entry_kernel[source], 0)
    rows_ky = ky_bank[kernel_of] * filled[:, None, None].astype(ky_bank.dtype)
    half_slice = jnp.einsum(
        "syp,spc->syc", rows_ky, slice_tiles[tile_of], preferred_element_type=jnp.float32
    ).astype(jnp.bfloat16)
    half_ctf = jnp.einsum(
        "syp,spc->syc", rows_ky, ctf_tiles[tile_of], preferred_element_type=jnp.float32
    ).astype(jnp.bfloat16)
    outgoing = jnp.concatenate([half_slice, half_ctf], axis=2)
    incoming, kind_ids = (
        lax.all_to_all(outgoing, ("img", "pen"), split_axis=0, concat_axis=0, tiled=True),
        lax.all_to_all(kernel_of, ("img", "pen"), split_axis=0, concat_axis=0, tiled=True),
    )
    plane_start = lax.axis_index("pen") * planes
    z_columns = lax.dynamic_slice_in_dim(z_bank, plane_start, planes, 1)
    onehot = (kind_ids[:, None] == jnp.arange(NK, dtype=jnp.int32)[None, :]).astype(jnp.bfloat16)
    mixing = (onehot[:, :, None] * z_columns[None, :, :]).reshape(slot_total, NK * planes)
    per_kernel = jnp.dot(
        mixing.T, incoming.reshape(slot_total, -1), preferred_element_type=jnp.float32
    )
    brick_sums = apply_kx(per_kernel, kx_bank).reshape(rows_brick, 3, planes, KXH)
    denominator = brick_sums[:, 2] + 1.0
    grid_real = brick_sums[:, 0] / denominator
    grid_imag = brick_sums[:, 1] / denominator
    quarter = NBOX // 4
    row_x = lax.broadcasted_iota(jnp.int32, (2 * NBOX, 2 * KXH), 0)
    col_x = lax.broadcasted_iota(jnp.int32, (2 * NBOX, 2 * KXH), 1)
    kx_of = col_x % KXH
    phase_x = (row_x // 2) * kx_of + quarter * (col_x // KXH - row_x % 2)
    table_x = jnp.where(kx_of == 0, 1.0, 2.0) * jnp.cos(
        2.0 * math.pi / NBOX * (phase_x % NBOX).astype(jnp.float32)
    )
    row_y = lax.broadcasted_iota(jnp.int32, (2 * NBOX, 2 * NBOX), 0)
    col_y = lax.broadcasted_iota(jnp.int32, (2 * NBOX, 2 * NBOX), 1)
    phase_y = (row_y // 2) * (col_y // 2) + quarter * (col_y % 2 - row_y % 2)
    table_y = jnp.cos(2.0 * math.pi / NBOX * (phase_y % NBOX).astype(jnp.float32))
    norm_scale = 1.0 / math.sqrt(window * NBOX * KXH)
    row_z = lax.broadcasted_iota(jnp.int32, (2 * window, ZW), 0)
    col_z = lax.broadcasted_iota(jnp.int32, (2 * window, ZW), 1)
    phase_z = (row_z // 2) * col_z + quarter * (row_z % 2)
    table_z = norm_scale * jnp.cos(2.0 * math.pi / NBOX * (phase_z % NBOX).astype(jnp.float32))
    table_x, table_y, table_z = lax.optimization_barrier((table_x, table_y, table_z))
    contract_minor = (((1,), (1,)), ((), ()))
    stacked = (
        jnp.concatenate([grid_real, grid_imag], axis=2)
        .transpose(1, 0, 2)
        .reshape(planes * rows_brick, 2 * KXH)
    )
    after_x = lax.dot_general(
        table_x, stacked, contract_minor, precision=lax.Precision.HIGH
    ).reshape(img_count, -1, planes * rows_brick)
    block_in = lax.all_to_all(after_x, "img", split_axis=0, concat_axis=0, tiled=True)
    x_local = NBOX // img_count
    rows_y = (
        block_in.reshape(img_count, x_local, 2, planes, rows_brick)
        .transpose(3, 1, 0, 4, 2)
        .reshape(planes * x_local, 2 * NBOX)
    )
    after_y = lax.dot_general(
        table_y, rows_y, contract_minor, precision=lax.Precision.HIGH
    ).reshape(pen_count, -1, planes * x_local)
    block_z = lax.all_to_all(after_y, "pen", split_axis=0, concat_axis=0, tiled=True)
    y_local = NBOX // pen_count
    rows_z = (
        block_z.reshape(pen_count, y_local, 2, planes, x_local)
        .transpose(1, 4, 0, 3, 2)
        .reshape(y_local * x_local, 2 * window)
    )
    volume = jnp.dot(rows_z, table_z, precision=lax.Precision.HIGH)
    return volume.reshape(y_local, x_local, ZW)

def solution(mesh):
    return jax.shard_map(
        local,
        mesh=mesh,
        in_specs=(
            P(("img", "pen"), None, None),
            P(("img", "pen"), None, None),
            P(("img", "pen")),
            P(("img", "pen"), None),
            P(("img", "pen")),
            P(),
            P(),
            P(),
        ),
        out_specs=P("pen", "img", None),
        check_vma=False,
    )
```

```python
import math

import jax
import jax.numpy as jnp
from jax import lax
from jax.experimental import pallas as pl
from jax.sharding import PartitionSpec as P

NBOX = 768
KXH = 384
PIX = 128
NK = 16
CAP = 2
ZW = 128


def angle_table(left_idx, right_idx):
    product = left_idx[:, None] * right_idx[None, :] % NBOX
    return 2.0 * math.pi / NBOX * product.astype(jnp.float32)


def kx_kernel(h_ref, w_ref, o_ref):
    @pl.when(pl.program_id(0) == 0)
    def _():
        o_ref[...] = jnp.zeros(o_ref.shape, o_ref.dtype)

    pix = w_ref.shape[1]
    h = jnp.concatenate(
        [h_ref[:, m * pix:(m + 1) * pix] for m in range(h_ref.shape[1] // pix)], axis=0
    )
    hi = h.astype(jnp.bfloat16)
    lo = (h - hi.astype(jnp.float32)).astype(jnp.bfloat16)
    w = w_ref[0]
    o_ref[...] += jnp.dot(hi, w, preferred_element_type=jnp.float32) + jnp.dot(
        lo, w, preferred_element_type=jnp.float32
    )


def apply_kx(per_kernel, kx_bank):
    kernels, pix, cols = kx_bank.shape
    planes = per_kernel.shape[0] // kernels
    width = per_kernel.shape[1]
    rows = planes * width // pix
    return pl.pallas_call(
        kx_kernel,
        grid=(kernels,),
        in_specs=[
            pl.BlockSpec((planes, width), lambda k: (k, 0)),
            pl.BlockSpec((1, pix, cols), lambda k: (k, 0, 0)),
        ],
        out_specs=pl.BlockSpec((rows, cols), lambda k: (0, 0)),
        out_shape=jax.ShapeDtypeStruct((rows, cols), jnp.float32),
    )(per_kernel, kx_bank)

def local(slice_tiles, ctf_tiles, entry_tile, entry_brick, entry_kernel, ky_bank, kx_bank, z_bank):
    img_count = lax.axis_size("img")
    pen_count = lax.axis_size("pen")
    bricks = img_count * pen_count
    entry_count = entry_tile.shape[0]
    rows_brick = ky_bank.shape[1]
    window = z_bank.shape[1]
    planes = window // pen_count
    slot_total = bricks * CAP
    target = entry_brick[:, 0]
    positions = jnp.arange(entry_count, dtype=jnp.int32)
    earlier = (target[None, :] == target[:, None]) & (positions[None, :] < positions[:, None])
    slot_rank = jnp.sum(earlier.astype(jnp.int32), axis=1)
    slot_index = target * CAP + slot_rank
    owner = jnp.full((slot_total,), entry_count, jnp.int32).at[slot_index].set(positions)
    filled = owner < entry_count
    source = jnp.minimum(owner, entry_count - 1)
    tile_of = entry_tile[source]
    kernel_of = jnp.where(filled, entry_kernel[source], 0)
    rows_ky = ky_bank[kernel_of] * filled[:, None, None].astype(ky_bank.dtype)
    pixels = jnp.concatenate([slice_tiles[tile_of], ctf_tiles[tile_of]], axis=2)
    outgoing = jnp.einsum(
        "syp,spc->syc", rows_ky, pixels, preferred_element_type=jnp.float32
    ).astype(jnp.bfloat16)
    incoming, kind_ids = (
        lax.all_to_all(outgoing, ("img", "pen"), split_axis=0, concat_axis=0, tiled=True),
        lax.all_to_all(kernel_of, ("img", "pen"), split_axis=0, concat_axis=0, tiled=True),
    )
    plane_start = lax.axis_index("pen") * planes
    z_columns = lax.dynamic_slice_in_dim(z_bank, plane_start, planes, 1)
    onehot = (kind_ids[:, None] == jnp.arange(NK, dtype=jnp.int32)[None, :]).astype(jnp.bfloat16)
    mixing = (onehot[:, :, None] * z_columns[None, :, :]).reshape(slot_total, NK * planes)
    per_kernel = jnp.dot(
        mixing.T, incoming.reshape(slot_total, -1), preferred_element_type=jnp.float32
    )
    brick_sums = apply_kx(per_kernel, kx_bank).reshape(rows_brick, 3, planes, KXH)
    denominator = brick_sums[:, 2] + 1.0
    grid_real = brick_sums[:, 0] / denominator
    grid_imag = brick_sums[:, 1] / denominator
    quarter = NBOX // 4
    row_x = lax.broadcasted_iota(jnp.int32, (2 * NBOX, 2 * KXH), 0)
    col_x = lax.broadcasted_iota(jnp.int32, (2 * NBOX, 2 * KXH), 1)
    kx_of = col_x % KXH
    phase_x = (row_x // 2) * kx_of + quarter * (col_x // KXH - row_x % 2)
    table_x = jnp.where(kx_of == 0, 1.0, 2.0) * jnp.cos(
        2.0 * math.pi / NBOX * (phase_x % NBOX).astype(jnp.float32)
    )
    row_y = lax.broadcasted_iota(jnp.int32, (2 * NBOX, 2 * NBOX), 0)
    col_y = lax.broadcasted_iota(jnp.int32, (2 * NBOX, 2 * NBOX), 1)
    phase_y = (row_y // 2) * (col_y // 2) + quarter * (col_y % 2 - row_y % 2)
    table_y = jnp.cos(2.0 * math.pi / NBOX * (phase_y % NBOX).astype(jnp.float32))
    norm_scale = 1.0 / math.sqrt(window * NBOX * KXH)
    row_z = lax.broadcasted_iota(jnp.int32, (2 * window, ZW), 0)
    col_z = lax.broadcasted_iota(jnp.int32, (2 * window, ZW), 1)
    phase_z = (row_z // 2) * col_z + quarter * (row_z % 2)
    table_z = norm_scale * jnp.cos(2.0 * math.pi / NBOX * (phase_z % NBOX).astype(jnp.float32))
    table_x, table_y, table_z = lax.optimization_barrier((table_x, table_y, table_z))
    contract_minor = (((1,), (1,)), ((), ()))
    stacked = (
        jnp.concatenate([grid_real, grid_imag], axis=2)
        .transpose(1, 0, 2)
        .reshape(planes * rows_brick, 2 * KXH)
    )
    after_x = lax.dot_general(
        table_x, stacked, contract_minor, precision=lax.Precision.HIGH
    ).reshape(img_count, -1, planes * rows_brick)
    block_in = lax.all_to_all(after_x, "img", split_axis=0, concat_axis=0, tiled=True)
    x_local = NBOX // img_count
    rows_y = (
        block_in.reshape(img_count, x_local, 2, planes, rows_brick)
        .transpose(3, 1, 0, 4, 2)
        .reshape(planes * x_local, 2 * NBOX)
    )
    after_y = lax.dot_general(
        table_y, rows_y, contract_minor, precision=lax.Precision.HIGH
    ).reshape(pen_count, -1, planes * x_local)
    block_z = lax.all_to_all(after_y, "pen", split_axis=0, concat_axis=0, tiled=True)
    y_local = NBOX // pen_count
    rows_z = (
        block_z.reshape(pen_count, y_local, 2, planes, x_local)
        .transpose(1, 4, 0, 3, 2)
        .reshape(y_local * x_local, 2 * window)
    )
    volume = jnp.dot(rows_z, table_z, precision=lax.Precision.HIGH)
    return volume.reshape(y_local, x_local, ZW)

def solution(mesh):
    return jax.shard_map(
        local,
        mesh=mesh,
        in_specs=(
            P(("img", "pen"), None, None),
            P(("img", "pen"), None, None),
            P(("img", "pen")),
            P(("img", "pen"), None),
            P(("img", "pen")),
            P(),
            P(),
            P(),
        ),
        out_specs=P("pen", "img", None),
        check_vma=False,
    )
```

```python
import math

import jax
import jax.numpy as jnp
from jax import lax
from jax.experimental import pallas as pl
from jax.sharding import PartitionSpec as P

NBOX = 768
KXH = 384
PIX = 128
NK = 16
CAP = 2
ZW = 128


def angle_table(left_idx, right_idx):
    product = left_idx[:, None] * right_idx[None, :] % NBOX
    return 2.0 * math.pi / NBOX * product.astype(jnp.float32)


def kx_kernel(h_ref, w_ref, o_ref):
    @pl.when(pl.program_id(0) == 0)
    def _():
        o_ref[...] = jnp.zeros(o_ref.shape, o_ref.dtype)

    rows, planes, _ = h_ref.shape
    pix = w_ref.shape[1]
    w = w_ref[0]
    for channel in range(o_ref.shape[0]):
        h = h_ref[:, :, channel * pix:(channel + 1) * pix].reshape(rows * planes, pix)
        hi = h.astype(jnp.bfloat16)
        lo = (h - hi.astype(jnp.float32)).astype(jnp.bfloat16)
        o_ref[channel] += jnp.dot(hi, w, preferred_element_type=jnp.float32) + jnp.dot(
            lo, w, preferred_element_type=jnp.float32
        )


def apply_kx(per_kernel, kx_bank):
    kernels, pix, cols = kx_bank.shape
    planes = per_kernel.shape[1] // kernels
    rows, width = per_kernel.shape[0], per_kernel.shape[2]
    channels = width // pix
    return pl.pallas_call(
        kx_kernel,
        grid=(kernels,),
        in_specs=[
            pl.BlockSpec((rows, planes, width), lambda k: (0, k, 0)),
            pl.BlockSpec((1, pix, cols), lambda k: (k, 0, 0)),
        ],
        out_specs=pl.BlockSpec((channels, planes * rows, cols), lambda k: (0, 0, 0)),
        out_shape=jax.ShapeDtypeStruct((channels, planes * rows, cols), jnp.float32),
    )(per_kernel, kx_bank)

def local(slice_tiles, ctf_tiles, entry_tile, entry_brick, entry_kernel, ky_bank, kx_bank, z_bank):
    img_count = lax.axis_size("img")
    pen_count = lax.axis_size("pen")
    bricks = img_count * pen_count
    entry_count = entry_tile.shape[0]
    rows_brick = ky_bank.shape[1]
    window = z_bank.shape[1]
    planes = window // pen_count
    slot_total = bricks * CAP
    target = entry_brick[:, 0]
    positions = jnp.arange(entry_count, dtype=jnp.int32)
    earlier = (target[None, :] == target[:, None]) & (positions[None, :] < positions[:, None])
    slot_rank = jnp.sum(earlier.astype(jnp.int32), axis=1)
    slot_index = target * CAP + slot_rank
    owner = jnp.full((slot_total,), entry_count, jnp.int32).at[slot_index].set(positions)
    filled = owner < entry_count
    source = jnp.minimum(owner, entry_count - 1)
    tile_of = entry_tile[source]
    kernel_of = jnp.where(filled, entry_kernel[source], 0)
    rows_ky = ky_bank[kernel_of] * filled[:, None, None].astype(ky_bank.dtype)
    pixels = jnp.concatenate([slice_tiles[tile_of], ctf_tiles[tile_of]], axis=2)
    outgoing = jnp.einsum(
        "syp,spc->syc", rows_ky, pixels, preferred_element_type=jnp.float32
    ).astype(jnp.bfloat16)
    incoming, kind_ids = (
        lax.all_to_all(outgoing, ("img", "pen"), split_axis=0, concat_axis=0, tiled=True),
        lax.all_to_all(kernel_of, ("img", "pen"), split_axis=0, concat_axis=0, tiled=True),
    )
    plane_start = lax.axis_index("pen") * planes
    z_columns = lax.dynamic_slice_in_dim(z_bank, plane_start, planes, 1)
    onehot = (kind_ids[:, None] == jnp.arange(NK, dtype=jnp.int32)[None, :]).astype(jnp.bfloat16)
    mixing = (onehot[:, :, None] * z_columns[None, :, :]).reshape(slot_total, NK * planes)
    per_kernel = lax.dot_general(
        mixing, incoming, (((0,), (0,)), ((), ())), preferred_element_type=jnp.float32
    ).transpose(1, 0, 2)
    brick_sums = apply_kx(per_kernel, kx_bank)
    denominator = brick_sums[2] + 1.0
    grid_real = brick_sums[0] / denominator
    grid_imag = brick_sums[1] / denominator
    quarter = NBOX // 4
    row_x = lax.broadcasted_iota(jnp.int32, (2 * NBOX, 2 * KXH), 0)
    col_x = lax.broadcasted_iota(jnp.int32, (2 * NBOX, 2 * KXH), 1)
    kx_of = col_x % KXH
    phase_x = (row_x // 2) * kx_of + quarter * (col_x // KXH - row_x % 2)
    table_x = jnp.where(kx_of == 0, 1.0, 2.0) * jnp.cos(
        2.0 * math.pi / NBOX * (phase_x % NBOX).astype(jnp.float32)
    )
    row_y = lax.broadcasted_iota(jnp.int32, (2 * NBOX, 2 * NBOX), 0)
    col_y = lax.broadcasted_iota(jnp.int32, (2 * NBOX, 2 * NBOX), 1)
    phase_y = (row_y // 2) * (col_y // 2) + quarter * (col_y % 2 - row_y % 2)
    table_y = jnp.cos(2.0 * math.pi / NBOX * (phase_y % NBOX).astype(jnp.float32))
    norm_scale = 1.0 / math.sqrt(window * NBOX * KXH)
    row_z = lax.broadcasted_iota(jnp.int32, (2 * window, ZW), 0)
    col_z = lax.broadcasted_iota(jnp.int32, (2 * window, ZW), 1)
    phase_z = (row_z // 2) * col_z + quarter * (row_z % 2)
    table_z = norm_scale * jnp.cos(2.0 * math.pi / NBOX * (phase_z % NBOX).astype(jnp.float32))
    table_x, table_y, table_z = lax.optimization_barrier((table_x, table_y, table_z))
    contract_minor = (((1,), (1,)), ((), ()))
    stacked = (
        jnp.concatenate([grid_real, grid_imag], axis=1)
        .reshape(rows_brick, planes, 2 * KXH)
        .transpose(1, 0, 2)
        .reshape(planes * rows_brick, 2 * KXH)
    )
    after_x = lax.dot_general(
        table_x, stacked, contract_minor, precision=lax.Precision.HIGH
    ).reshape(img_count, -1, planes * rows_brick)
    block_in = lax.all_to_all(after_x, "img", split_axis=0, concat_axis=0, tiled=True)
    x_local = NBOX // img_count
    rows_y = (
        block_in.reshape(img_count, x_local, 2, planes, rows_brick)
        .transpose(3, 1, 0, 4, 2)
        .reshape(planes * x_local, 2 * NBOX)
    )
    after_y = lax.dot_general(
        table_y, rows_y, contract_minor, precision=lax.Precision.HIGH
    ).reshape(pen_count, -1, planes * x_local)
    block_z = lax.all_to_all(after_y, "pen", split_axis=0, concat_axis=0, tiled=True)
    y_local = NBOX // pen_count
    rows_z = (
        block_z.reshape(pen_count, y_local, 2, planes, x_local)
        .transpose(1, 4, 0, 3, 2)
        .reshape(y_local * x_local, 2 * window)
    )
    volume = jnp.dot(rows_z, table_z, precision=lax.Precision.HIGH)
    return volume.reshape(y_local, x_local, ZW)

def solution(mesh):
    return jax.shard_map(
        local,
        mesh=mesh,
        in_specs=(
            P(("img", "pen"), None, None),
            P(("img", "pen"), None, None),
            P(("img", "pen")),
            P(("img", "pen"), None),
            P(("img", "pen")),
            P(),
            P(),
            P(),
        ),
        out_specs=P("pen", "img", None),
        check_vma=False,
    )
```

```python
import math

import jax
import jax.numpy as jnp
from jax import lax
from jax.experimental import pallas as pl
from jax.sharding import PartitionSpec as P

NBOX = 768
KXH = 384
PIX = 128
NK = 16
CAP = 2
ZW = 128


def angle_table(left_idx, right_idx):
    product = left_idx[:, None] * right_idx[None, :] % NBOX
    return 2.0 * math.pi / NBOX * product.astype(jnp.float32)


def kx_kernel(h_ref, w_ref, o_ref):
    @pl.when(pl.program_id(0) == 0)
    def _():
        o_ref[...] = jnp.zeros(o_ref.shape, o_ref.dtype)

    rows, planes, _ = h_ref.shape
    pix = w_ref.shape[1]
    w = w_ref[0]
    for channel in range(o_ref.shape[0]):
        h = h_ref[:, :, channel * pix:(channel + 1) * pix].reshape(rows * planes, pix)
        hi = h.astype(jnp.bfloat16)
        lo = (h - hi.astype(jnp.float32)).astype(jnp.bfloat16)
        o_ref[channel] += jnp.dot(hi, w, preferred_element_type=jnp.float32) + jnp.dot(
            lo, w, preferred_element_type=jnp.float32
        )


def apply_kx(per_kernel, kx_bank):
    kernels, pix, cols = kx_bank.shape
    planes = per_kernel.shape[1] // kernels
    rows, width = per_kernel.shape[0], per_kernel.shape[2]
    channels = width // pix
    return pl.pallas_call(
        kx_kernel,
        grid=(kernels,),
        in_specs=[
            pl.BlockSpec((rows, planes, width), lambda k: (0, k, 0)),
            pl.BlockSpec((1, pix, cols), lambda k: (k, 0, 0)),
        ],
        out_specs=pl.BlockSpec((channels, planes * rows, cols), lambda k: (0, 0, 0)),
        out_shape=jax.ShapeDtypeStruct((channels, planes * rows, cols), jnp.float32),
    )(per_kernel, kx_bank)

def local(slice_tiles, ctf_tiles, entry_tile, entry_brick, entry_kernel, ky_bank, kx_bank, z_bank):
    img_count = lax.axis_size("img")
    pen_count = lax.axis_size("pen")
    bricks = img_count * pen_count
    entry_count = entry_tile.shape[0]
    rows_brick = ky_bank.shape[1]
    window = z_bank.shape[1]
    planes = window // pen_count
    slot_total = bricks * CAP
    target = entry_brick[:, 0]
    positions = jnp.arange(entry_count, dtype=jnp.int32)
    earlier = (target[None, :] == target[:, None]) & (positions[None, :] < positions[:, None])
    slot_rank = jnp.sum(earlier.astype(jnp.int32), axis=1)
    slot_index = target * CAP + slot_rank
    owner = jnp.full((slot_total,), entry_count, jnp.int32).at[slot_index].set(positions)
    filled = owner < entry_count
    source = jnp.minimum(owner, entry_count - 1)
    pixels = jnp.concatenate([slice_tiles[entry_tile], ctf_tiles[entry_tile]], axis=2)
    half_tile = jnp.einsum(
        "eyp,epc->eyc", ky_bank[entry_kernel], pixels, preferred_element_type=jnp.float32
    ).astype(jnp.bfloat16)
    kernel_of = jnp.where(filled, entry_kernel[source], 0)
    outgoing = jnp.where(filled[:, None, None], half_tile[source], jnp.zeros((), jnp.bfloat16))
    incoming, kind_ids = (
        lax.all_to_all(outgoing, ("img", "pen"), split_axis=0, concat_axis=0, tiled=True),
        lax.all_to_all(kernel_of, ("img", "pen"), split_axis=0, concat_axis=0, tiled=True),
    )
    plane_start = lax.axis_index("pen") * planes
    z_columns = lax.dynamic_slice_in_dim(z_bank, plane_start, planes, 1)
    onehot = (kind_ids[:, None] == jnp.arange(NK, dtype=jnp.int32)[None, :]).astype(jnp.bfloat16)
    mixing = (onehot[:, :, None] * z_columns[None, :, :]).reshape(slot_total, NK * planes)
    per_kernel = lax.dot_general(
        mixing, incoming, (((0,), (0,)), ((), ())), preferred_element_type=jnp.float32
    ).transpose(1, 0, 2)
    brick_sums = apply_kx(per_kernel, kx_bank)
    denominator = brick_sums[2] + 1.0
    grid_real = brick_sums[0] / denominator
    grid_imag = brick_sums[1] / denominator
    quarter = NBOX // 4
    row_x = lax.broadcasted_iota(jnp.int32, (2 * NBOX, 2 * KXH), 0)
    col_x = lax.broadcasted_iota(jnp.int32, (2 * NBOX, 2 * KXH), 1)
    kx_of = col_x % KXH
    phase_x = (row_x // 2) * kx_of + quarter * (col_x // KXH - row_x % 2)
    table_x = jnp.where(kx_of == 0, 1.0, 2.0) * jnp.cos(
        2.0 * math.pi / NBOX * (phase_x % NBOX).astype(jnp.float32)
    )
    row_y = lax.broadcasted_iota(jnp.int32, (2 * NBOX, 2 * NBOX), 0)
    col_y = lax.broadcasted_iota(jnp.int32, (2 * NBOX, 2 * NBOX), 1)
    phase_y = (row_y // 2) * (col_y // 2) + quarter * (col_y % 2 - row_y % 2)
    table_y = jnp.cos(2.0 * math.pi / NBOX * (phase_y % NBOX).astype(jnp.float32))
    norm_scale = 1.0 / math.sqrt(window * NBOX * KXH)
    row_z = lax.broadcasted_iota(jnp.int32, (2 * window, ZW), 0)
    col_z = lax.broadcasted_iota(jnp.int32, (2 * window, ZW), 1)
    phase_z = (row_z // 2) * col_z + quarter * (row_z % 2)
    table_z = norm_scale * jnp.cos(2.0 * math.pi / NBOX * (phase_z % NBOX).astype(jnp.float32))
    table_x, table_y, table_z = lax.optimization_barrier((table_x, table_y, table_z))
    contract_minor = (((1,), (1,)), ((), ()))
    stacked = (
        jnp.concatenate([grid_real, grid_imag], axis=1)
        .reshape(rows_brick, planes, 2 * KXH)
        .transpose(1, 0, 2)
        .reshape(planes * rows_brick, 2 * KXH)
    )
    after_x = lax.dot_general(
        table_x, stacked, contract_minor, precision=lax.Precision.HIGH
    ).reshape(img_count, -1, planes * rows_brick)
    block_in = lax.all_to_all(after_x, "img", split_axis=0, concat_axis=0, tiled=True)
    x_local = NBOX // img_count
    rows_y = (
        block_in.reshape(img_count, x_local, 2, planes, rows_brick)
        .transpose(3, 1, 0, 4, 2)
        .reshape(planes * x_local, 2 * NBOX)
    )
    after_y = lax.dot_general(
        table_y, rows_y, contract_minor, precision=lax.Precision.HIGH
    ).reshape(pen_count, -1, planes * x_local)
    block_z = lax.all_to_all(after_y, "pen", split_axis=0, concat_axis=0, tiled=True)
    y_local = NBOX // pen_count
    rows_z = (
        block_z.reshape(pen_count, y_local, 2, planes, x_local)
        .transpose(1, 4, 0, 3, 2)
        .reshape(y_local * x_local, 2 * window)
    )
    volume = jnp.dot(rows_z, table_z, precision=lax.Precision.HIGH)
    return volume.reshape(y_local, x_local, ZW)

def solution(mesh):
    return jax.shard_map(
        local,
        mesh=mesh,
        in_specs=(
            P(("img", "pen"), None, None),
            P(("img", "pen"), None, None),
            P(("img", "pen")),
            P(("img", "pen"), None),
            P(("img", "pen")),
            P(),
            P(),
            P(),
        ),
        out_specs=P("pen", "img", None),
        check_vma=False,
    )
```

```python
import math

import jax
import numpy as np
import jax.numpy as jnp
from jax import lax
from jax.experimental import pallas as pl
from jax.sharding import PartitionSpec as P

NBOX = 768
KXH = 384
PIX = 128
NK = 16
CAP = 2
ZW = 128


def angle_table(left_idx, right_idx):
    product = left_idx[:, None] * right_idx[None, :] % NBOX
    return 2.0 * math.pi / NBOX * product.astype(jnp.float32)


def kx_kernel(h_ref, w_ref, o_ref):
    @pl.when(pl.program_id(0) == 0)
    def _():
        o_ref[...] = jnp.zeros(o_ref.shape, o_ref.dtype)

    rows, planes, _ = h_ref.shape
    pix = w_ref.shape[1]
    w = w_ref[0]
    for channel in range(o_ref.shape[0]):
        h = h_ref[:, :, channel * pix:(channel + 1) * pix].reshape(rows * planes, pix)
        hi = h.astype(jnp.bfloat16)
        lo = (h - hi.astype(jnp.float32)).astype(jnp.bfloat16)
        o_ref[channel] += jnp.dot(hi, w, preferred_element_type=jnp.float32) + jnp.dot(
            lo, w, preferred_element_type=jnp.float32
        )


def apply_kx(per_kernel, kx_bank):
    kernels, pix, cols = kx_bank.shape
    planes = per_kernel.shape[1] // kernels
    rows, width = per_kernel.shape[0], per_kernel.shape[2]
    channels = width // pix
    return pl.pallas_call(
        kx_kernel,
        grid=(kernels,),
        in_specs=[
            pl.BlockSpec((rows, planes, width), lambda k: (0, k, 0)),
            pl.BlockSpec((1, pix, cols), lambda k: (k, 0, 0)),
        ],
        out_specs=pl.BlockSpec((channels, planes * rows, cols), lambda k: (0, 0, 0)),
        out_shape=jax.ShapeDtypeStruct((channels, planes * rows, cols), jnp.float32),
    )(per_kernel, kx_bank)

def dft_tables(window):
    quarter = NBOX // 4
    row_x, col_x = np.indices((2 * NBOX, 2 * KXH))
    kx_of = col_x % KXH
    phase_x = ((row_x // 2) * kx_of + quarter * (col_x // KXH - row_x % 2)) % NBOX
    table_x = np.where(kx_of == 0, 1.0, 2.0) * np.cos(2.0 * np.pi / NBOX * phase_x)
    row_y, col_y = np.indices((2 * NBOX, 2 * NBOX))
    phase_y = ((row_y // 2) * (col_y // 2) + quarter * (col_y % 2 - row_y % 2)) % NBOX
    table_y = np.cos(2.0 * np.pi / NBOX * phase_y)
    row_z, col_z = np.indices((2 * window, ZW))
    phase_z = ((row_z // 2) * col_z + quarter * (row_z % 2)) % NBOX
    table_z = np.cos(2.0 * np.pi / NBOX * phase_z) / math.sqrt(window * NBOX * KXH)
    return tuple(jnp.asarray(t, jnp.float32) for t in (table_x, table_y, table_z))


def local(slice_tiles, ctf_tiles, entry_tile, entry_brick, entry_kernel, ky_bank, kx_bank, z_bank):
    img_count = lax.axis_size("img")
    pen_count = lax.axis_size("pen")
    bricks = img_count * pen_count
    entry_count = entry_tile.shape[0]
    rows_brick = ky_bank.shape[1]
    window = z_bank.shape[1]
    planes = window // pen_count
    slot_total = bricks * CAP
    target = entry_brick[:, 0]
    positions = jnp.arange(entry_count, dtype=jnp.int32)
    earlier = (target[None, :] == target[:, None]) & (positions[None, :] < positions[:, None])
    slot_rank = jnp.sum(earlier.astype(jnp.int32), axis=1)
    slot_index = target * CAP + slot_rank
    owner = jnp.full((slot_total,), entry_count, jnp.int32).at[slot_index].set(positions)
    owner = owner.reshape(bricks, CAP)
    pixels = jnp.concatenate([slice_tiles[entry_tile], ctf_tiles[entry_tile]], axis=2)
    half_tile = jnp.einsum(
        "eyp,epc->eyc", ky_bank[entry_kernel], pixels, preferred_element_type=jnp.float32
    ).astype(jnp.bfloat16)
    plane_start = lax.axis_index("pen") * planes
    z_columns = lax.dynamic_slice_in_dim(z_bank, plane_start, planes, 1)
    per_kernel = None
    for rank in range(CAP):
        owned = owner[:, rank]
        filled = owned < entry_count
        source = jnp.minimum(owned, entry_count - 1)
        kernel_of = jnp.where(filled, entry_kernel[source], 0)
        outgoing = jnp.where(filled[:, None, None], half_tile[source], jnp.zeros((), jnp.bfloat16))
        incoming, kind_ids = (
            lax.all_to_all(outgoing, ("img", "pen"), split_axis=0, concat_axis=0, tiled=True),
            lax.all_to_all(kernel_of, ("img", "pen"), split_axis=0, concat_axis=0, tiled=True),
        )
        onehot = (kind_ids[:, None] == jnp.arange(NK, dtype=jnp.int32)[None, :]).astype(jnp.bfloat16)
        mixing = (onehot[:, :, None] * z_columns[None, :, :]).reshape(bricks, NK * planes)
        part = lax.dot_general(
            mixing, incoming, (((0,), (0,)), ((), ())), preferred_element_type=jnp.float32
        ).transpose(1, 0, 2)
        per_kernel = part if per_kernel is None else per_kernel + part
    brick_sums = apply_kx(per_kernel, kx_bank)
    denominator = brick_sums[2] + 1.0
    grid_real = brick_sums[0] / denominator
    grid_imag = brick_sums[1] / denominator
    table_x, table_y, table_z = dft_tables(window)
    contract_minor = (((1,), (1,)), ((), ()))
    stacked = (
        jnp.concatenate([grid_real, grid_imag], axis=1)
        .reshape(rows_brick, planes, 2 * KXH)
        .transpose(1, 0, 2)
        .reshape(planes * rows_brick, 2 * KXH)
    )
    after_x = lax.dot_general(
        table_x, stacked, contract_minor, precision=lax.Precision.HIGH
    ).reshape(img_count, -1, planes * rows_brick)
    block_in = lax.all_to_all(after_x, "img", split_axis=0, concat_axis=0, tiled=True)
    x_local = NBOX // img_count
    rows_y = (
        block_in.reshape(img_count, x_local, 2, planes, rows_brick)
        .transpose(3, 1, 0, 4, 2)
        .reshape(planes * x_local, 2 * NBOX)
    )
    after_y = lax.dot_general(
        table_y, rows_y, contract_minor, precision=lax.Precision.HIGH
    ).reshape(pen_count, -1, planes * x_local)
    block_z = lax.all_to_all(after_y, "pen", split_axis=0, concat_axis=0, tiled=True)
    y_local = NBOX // pen_count
    rows_z = (
        block_z.reshape(pen_count, y_local, 2, planes, x_local)
        .transpose(1, 4, 0, 3, 2)
        .reshape(y_local * x_local, 2 * window)
    )
    volume = jnp.dot(rows_z, table_z, precision=lax.Precision.HIGH)
    return volume.reshape(y_local, x_local, ZW)

def solution(mesh):
    return jax.shard_map(
        local,
        mesh=mesh,
        in_specs=(
            P(("img", "pen"), None, None),
            P(("img", "pen"), None, None),
            P(("img", "pen")),
            P(("img", "pen"), None),
            P(("img", "pen")),
            P(),
            P(),
            P(),
        ),
        out_specs=P("pen", "img", None),
        check_vma=False,
    )
```

```python
import math

import jax
import jax.numpy as jnp
from jax import lax
from jax.experimental import pallas as pl
from jax.sharding import PartitionSpec as P

NBOX = 768
KXH = 384
PIX = 128
NK = 16
CAP = 2
ZW = 128


def angle_table(left_idx, right_idx):
    product = left_idx[:, None] * right_idx[None, :] % NBOX
    return 2.0 * math.pi / NBOX * product.astype(jnp.float32)


def kx_kernel(h_ref, w_ref, o_ref):
    @pl.when(pl.program_id(0) == 0)
    def _():
        o_ref[...] = jnp.zeros(o_ref.shape, o_ref.dtype)

    rows, planes, _ = h_ref.shape
    pix = w_ref.shape[1]
    w = w_ref[0]
    for channel in range(o_ref.shape[0]):
        h = h_ref[:, :, channel * pix:(channel + 1) * pix].reshape(rows * planes, pix)
        hi = h.astype(jnp.bfloat16)
        lo = (h - hi.astype(jnp.float32)).astype(jnp.bfloat16)
        o_ref[channel] += jnp.dot(hi, w, preferred_element_type=jnp.float32) + jnp.dot(
            lo, w, preferred_element_type=jnp.float32
        )


def apply_kx(per_kernel, kx_bank):
    kernels, pix, cols = kx_bank.shape
    planes = per_kernel.shape[1] // kernels
    rows, width = per_kernel.shape[0], per_kernel.shape[2]
    channels = width // pix
    return pl.pallas_call(
        kx_kernel,
        grid=(kernels,),
        in_specs=[
            pl.BlockSpec((rows, planes, width), lambda k: (0, k, 0)),
            pl.BlockSpec((1, pix, cols), lambda k: (k, 0, 0)),
        ],
        out_specs=pl.BlockSpec((channels, planes * rows, cols), lambda k: (0, 0, 0)),
        out_shape=jax.ShapeDtypeStruct((channels, planes * rows, cols), jnp.float32),
    )(per_kernel, kx_bank)

def local(slice_tiles, ctf_tiles, entry_tile, entry_brick, entry_kernel, ky_bank, kx_bank, z_bank):
    img_count = lax.axis_size("img")
    pen_count = lax.axis_size("pen")
    bricks = img_count * pen_count
    entry_count = entry_tile.shape[0]
    rows_brick = ky_bank.shape[1]
    window = z_bank.shape[1]
    planes = window // pen_count
    slot_total = bricks * CAP
    target = entry_brick[:, 0]
    positions = jnp.arange(entry_count, dtype=jnp.int32)
    earlier = (target[None, :] == target[:, None]) & (positions[None, :] < positions[:, None])
    slot_rank = jnp.sum(earlier.astype(jnp.int32), axis=1)
    slot_index = target * CAP + slot_rank
    owner = jnp.full((slot_total,), entry_count, jnp.int32).at[slot_index].set(positions)
    filled = owner < entry_count
    source = jnp.minimum(owner, entry_count - 1)
    pixels = jnp.concatenate([slice_tiles[entry_tile], ctf_tiles[entry_tile]], axis=2)
    half_tile = jnp.einsum(
        "eyp,epc->eyc", ky_bank[entry_kernel], pixels, preferred_element_type=jnp.float32
    ).astype(jnp.bfloat16)
    kernel_of = jnp.where(filled, entry_kernel[source], 0)
    outgoing = jnp.where(filled[:, None, None], half_tile[source], jnp.zeros((), jnp.bfloat16))
    incoming, kind_ids = (
        lax.all_to_all(outgoing, ("img", "pen"), split_axis=0, concat_axis=0, tiled=True),
        lax.all_to_all(kernel_of, ("img", "pen"), split_axis=0, concat_axis=0, tiled=True),
    )
    plane_start = lax.axis_index("pen") * planes
    z_columns = lax.dynamic_slice_in_dim(z_bank, plane_start, planes, 1)
    onehot = (kind_ids[:, None] == jnp.arange(NK, dtype=jnp.int32)[None, :]).astype(jnp.bfloat16)
    mixing = (onehot[:, :, None] * z_columns[None, :, :]).reshape(slot_total, NK * planes)
    per_kernel = lax.dot_general(
        mixing, incoming, (((0,), (0,)), ((), ())), preferred_element_type=jnp.float32
    ).transpose(1, 0, 2)
    brick_sums = apply_kx(per_kernel, kx_bank)
    denominator = brick_sums[2] + 1.0
    grid_real = brick_sums[0] / denominator
    grid_imag = brick_sums[1] / denominator
    quarter = NBOX // 4
    row_x = lax.broadcasted_iota(jnp.int32, (2 * NBOX, 2 * KXH), 0)
    col_x = lax.broadcasted_iota(jnp.int32, (2 * NBOX, 2 * KXH), 1)
    kx_of = col_x % KXH
    phase_x = (row_x // 2) * kx_of + quarter * (col_x // KXH - row_x % 2)
    table_x = jnp.where(kx_of == 0, 1.0, 2.0) * jnp.cos(
        2.0 * math.pi / NBOX * (phase_x % NBOX).astype(jnp.float32)
    )
    row_y = lax.broadcasted_iota(jnp.int32, (2 * NBOX, 2 * NBOX), 0)
    col_y = lax.broadcasted_iota(jnp.int32, (2 * NBOX, 2 * NBOX), 1)
    phase_y = (row_y // 2) * (col_y // 2) + quarter * (col_y % 2 - row_y % 2)
    table_y = jnp.cos(2.0 * math.pi / NBOX * (phase_y % NBOX).astype(jnp.float32))
    norm_scale = 1.0 / math.sqrt(window * NBOX * KXH)
    row_z = lax.broadcasted_iota(jnp.int32, (2 * window, ZW), 0)
    col_z = lax.broadcasted_iota(jnp.int32, (2 * window, ZW), 1)
    phase_z = (row_z // 2) * col_z + quarter * (row_z % 2)
    table_z = norm_scale * jnp.cos(2.0 * math.pi / NBOX * (phase_z % NBOX).astype(jnp.float32))
    table_x, table_y, table_z = lax.optimization_barrier((table_x, table_y, table_z))
    contract_minor = (((1,), (1,)), ((), ()))
    stacked = (
        jnp.concatenate([grid_real, grid_imag], axis=1)
        .reshape(rows_brick, planes, 2 * KXH)
        .transpose(1, 0, 2)
        .reshape(planes * rows_brick, 2 * KXH)
    )
    after_x = lax.dot_general(
        table_x, stacked, contract_minor, precision=lax.Precision.HIGH
    ).reshape(img_count, -1, planes * rows_brick)
    block_in = lax.all_to_all(after_x, "img", split_axis=0, concat_axis=0, tiled=True)
    x_local = NBOX // img_count
    rows_y = (
        block_in.reshape(img_count, x_local, 2, planes, rows_brick)
        .transpose(3, 1, 0, 4, 2)
        .reshape(planes * x_local, 2 * NBOX)
    )
    after_y = lax.dot_general(
        table_y, rows_y, contract_minor, precision=lax.Precision.HIGH
    ).reshape(pen_count, -1, planes * x_local)
    block_z = lax.all_to_all(after_y, "pen", split_axis=0, concat_axis=0, tiled=True)
    y_local = NBOX // pen_count
    blocks_z = block_z.reshape(pen_count, y_local, 2, planes, x_local)
    weights_z = table_z.reshape(pen_count, planes, 2, ZW)
    return jnp.einsum("pyekx,pkez->yxz", blocks_z, weights_z, precision=lax.Precision.HIGH)

def solution(mesh):
    return jax.shard_map(
        local,
        mesh=mesh,
        in_specs=(
            P(("img", "pen"), None, None),
            P(("img", "pen"), None, None),
            P(("img", "pen")),
            P(("img", "pen"), None),
            P(("img", "pen")),
            P(),
            P(),
            P(),
        ),
        out_specs=P("pen", "img", None),
        check_vma=False,
    )
```
